32 devices in a mesh: batch: 4 (over y, x), dom: 8 (over z, core).
Axes of the slice: x: 2, y: 2, z: 4, core: 2. Of those that a mesh axis runs over, the one named last changes fastest.
Arguments:
- cell_feat: bfloat16 [4, 4096, 256], P('batch', 'dom'), may hold values from -6 to 6
- net_feat: bfloat16 [4, 4096, 256], P('batch', 'dom'), may hold values from -6 to 6
- net_grad: bfloat16 [4, 4096, 256], P('batch', 'dom'), may hold values from -6 to 6
- w_first: bfloat16 [512, 512], replicated, may hold values from -0.25 to 0.25
- w_second: bfloat16 [512, 256], replicated, may hold values from -0.25 to 0.25
- pin_cell: int32 [4, 8, 8, 256], P('batch', 'dom'), may hold values from 0 to 511
- pin_net: int32 [4, 8, 8, 256], P('batch', 'dom'), may hold values from 0 to 511
- pin_count: int32 [4, 8, 8], P('batch', 'dom'), may hold values from 224 to 256, as said below
Outputs:
- cell_out: float32 [4, 4096, 256], P('batch', 'dom')
- net_out: float32 [4, 4096, 256], P('batch', 'dom')
- first_total: float32 [512, 512], replicated
- second_total: float32 [512, 256], replicated
The draws below stay inside these ranges and needn't reach their ends.
Inputs may be any that keep to these rules, and one draw needn't show every extreme that they name: `pin_count`: every partition sends at most 256 live slots to each owner, and in every design each partition fills its slots to some owner.
All inputs are finite; a program needn't handle non-finite values.
Results may differ from the reference program's by a relative error of at most 0.004.
Values may be sent and summed in bfloat16 or wider, within the bound.
A program may use at most 64 MiB of HBM per device.

```python
import math
import jax
import jax.numpy as jnp
import numpy as np
from jax import lax

H = 256
IN = 512
MID = 512
SLOT_DEV = 2048
CAP = 256
CELL_DEV = 512
NET_DEV = 512
DESIGNS = 4
CELLS = 4096
NETS = 4096
N_DOM = 8


def draw_pin_count(key, part):
    base_key = jax.random.fold_in(key, 7)
    first_key, second_key = jax.random.split(base_key)
    lowest = CAP - max(1, CAP // 8)
    base = jax.random.randint(first_key, (DESIGNS, N_DOM, N_DOM), lowest, CAP + 1)
    picked = jax.random.randint(second_key, (DESIGNS, N_DOM, 1), 0, N_DOM)
    column = lax.broadcasted_iota(jnp.int32, (DESIGNS, N_DOM, N_DOM), 2)
    return jnp.where(column == picked, CAP, base).astype(jnp.int32)


def plant(values, own_key, least, high):
    index_at = [jax.random.randint(jax.random.fold_in(own_key, axis), (), 0, length) for axis, length in enumerate(values.shape)]
    main_axis = values.shape.index(max(values.shape))
    next_to = index_at[:main_axis] + [(index_at[main_axis] + 1) % values.shape[main_axis]] + index_at[main_axis + 1:]
    return values.at[tuple(index_at)].set(least).at[tuple(next_to)].set(high)


def block_levels(key, extent, cuts, smallest, top_value):
    def one(axis_at, blocks):
        steps = jax.random.uniform(jax.random.fold_in(jax.random.fold_in(key, 6), axis_at), (blocks,), jnp.float32, smallest / len(cuts), top_value / len(cuts))
        return jnp.repeat(jnp.exp(steps), extent[axis_at] // blocks).reshape((-1,) + (1,) * (len(extent) - axis_at - 1))

    gain = one(*cuts[0])
    for cut in cuts[1:]:
        gain = gain * one(*cut)
    return gain


def rank_bounds(number_of, lean):
    portions = [(1 << 20) // math.isqrt(rank ** lean) + 1 for rank in range(1, number_of + 1)]
    deviation = 1 + sum(portions) // (1 << 30)
    return np.cumsum(np.array([max(1, weight // deviation) for weight in portions]))


def ranked_ids(rng, dims, number_of, slope):
    listing = rank_bounds(number_of, slope)
    ticket = jax.random.randint(jax.random.fold_in(rng, 1), dims, 0, int(listing[number_of - 1]))
    grade = jnp.searchsorted(jnp.asarray(listing, jnp.int32), ticket, side="right")
    return jax.random.permutation(jax.random.fold_in(rng, 2), number_of)[grade].astype(jnp.int32)


def bell_draw(rng, dims, deviation, reach, pieces=(), kind=jnp.bfloat16):
    array = jax.random.normal(rng, dims, jnp.float32) * deviation
    if len(pieces) > 0:
        array = block_levels(rng, dims, pieces, -0.22, 0.18) * array
    return jnp.clip(array, min=-reach, max=reach).astype(kind)


def setup_inputs(seed: int = 0) -> dict:
    seeds = jax.random.split(jax.random.key(seed), 9)
    cell_feat = bell_draw(seeds[0], (DESIGNS, CELLS, H), 1.0, 6.0, ((0, 4), (1, 8)))
    net_feat = bell_draw(seeds[1], (DESIGNS, NETS, H), 1.0, 6.0, ((0, 4), (1, 8)))
    net_grad = bell_draw(seeds[2], (DESIGNS, NETS, H), 1.0, 6.0, ((0, 4), (1, 8)))
    w_first = bell_draw(seeds[3], (IN, MID), IN ** -0.5, 0.25)
    w_second = bell_draw(seeds[4], (MID, H), MID ** -0.5, 0.25)
    pin_cell = plant(jax.random.randint(seeds[5], (DESIGNS, N_DOM, N_DOM, CAP), 0, CELL_DEV), jax.random.fold_in(seeds[5], 1), 0, CELL_DEV - 1).astype(jnp.int32)
    pin_net = plant(ranked_ids(seeds[6], (DESIGNS, N_DOM, N_DOM, CAP), NET_DEV, 1), jax.random.fold_in(seeds[6], 3), 0, NET_DEV - 1).astype(jnp.int32)
    pin_count = draw_pin_count(jax.random.fold_in(seeds[8], 71), 0)
    return dict(cell_feat=cell_feat, net_feat=net_feat, net_grad=net_grad, w_first=w_first, w_second=w_second, pin_cell=pin_cell, pin_net=pin_net, pin_count=pin_count)


def backward_core(pin_input, pin_grad, w_first, w_second):
    pre_act = jnp.dot(pin_input, w_first, preferred_element_type=jnp.float32)
    hidden = jax.nn.silu(pre_act).astype(jnp.bfloat16)
    second_part = lax.dot_general(hidden, pin_grad, (((0,), (0,)), ((), ())), preferred_element_type=jnp.float32)
    hidden_grad = lax.dot_general(pin_grad, w_second, (((1,), (1,)), ((), ())), preferred_element_type=jnp.float32)
    gate_sig = jax.nn.sigmoid(pre_act)
    pre_grad = (hidden_grad * gate_sig * (1.0 + pre_act * (1.0 - gate_sig))).astype(jnp.bfloat16)
    first_part = lax.dot_general(pin_input, pre_grad, (((0,), (0,)), ((), ())), preferred_element_type=jnp.float32)
    input_grad = lax.dot_general(pre_grad, w_first, (((1,), (1,)), ((), ())), preferred_element_type=jnp.float32).astype(jnp.bfloat16)
    return (input_grad, first_part, second_part)

def reference(cell_feat, net_feat, net_grad, w_first, w_second, pin_cell, pin_net, pin_count):
    shape_slots = (N_DOM, N_DOM, CAP)
    source = lax.broadcasted_iota(jnp.int32, shape_slots, 0)
    owner = lax.broadcasted_iota(jnp.int32, shape_slots, 1)
    position = lax.broadcasted_iota(jnp.int32, shape_slots, 2)

    def per_design(carry, item):
        cell_table, net_table, grad_table, slot_cell, slot_net, counts = item
        is_live = (position < counts[:, :, None]).reshape(-1)
        cell_index = (source * CELL_DEV + slot_cell).reshape(-1).astype(jnp.int32)
        net_index = (owner * NET_DEV + slot_net).reshape(-1).astype(jnp.int32)
        pin_input = jnp.concatenate([jnp.take(cell_table, cell_index, axis=0), jnp.take(net_table, net_index, axis=0)], axis=1)
        pin_grad = jnp.where(is_live[:, None], jnp.take(grad_table, net_index, axis=0), jnp.zeros((), jnp.bfloat16))
        input_grad, first_part, second_part = backward_core(pin_input, pin_grad, w_first, w_second)
        cell_part = jax.ops.segment_sum(input_grad[:, :H].astype(jnp.float32), cell_index, num_segments=CELLS)
        net_part = jax.ops.segment_sum(input_grad[:, H:].astype(jnp.float32), net_index, num_segments=NETS)
        return ((carry[0] + first_part, carry[1] + second_part), (cell_part, net_part))
    start = (jnp.zeros((IN, MID), jnp.float32), jnp.zeros((MID, H), jnp.float32))
    sums, outs = lax.scan(per_design, start, (cell_feat, net_feat, net_grad, pin_cell, pin_net, pin_count))
    wgrad_scale = 1.0 / math.sqrt(DESIGNS * N_DOM * SLOT_DEV)
    return (outs[0], outs[1], sums[0] * wgrad_scale, sums[1] * wgrad_scale)
```

```python
import functools
import math

import jax
import jax.numpy as jnp
from jax import lax
from jax.experimental import pallas as pl
from jax.experimental.pallas import tpu as pltpu
from jax.sharding import PartitionSpec as P

BF = jnp.bfloat16
F32 = jnp.float32
MESH = pl.DeviceIdType.MESH
TAB_CHUNKS = 4
GRAD_CHUNKS = 4


def mm(a, b):
    return jnp.dot(a, b, preferred_element_type=F32)


def mm_t(a, b):
    return lax.dot_general(a, b, (((1,), (1,)), ((), ())), preferred_element_type=F32)


def one_hot_t(row, count):
    at = lax.broadcasted_iota(jnp.int32, (count, row.shape[1]), 0)
    return jnp.where(at == row, 1.0, 0.0).astype(BF)


def kernel(
    batches, depth, rows_z,
    cell_hbm, net_hbm, grad_hbm, w1_hbm, w2_hbm, cell_pin_hbm, net_pin_hbm, count_hbm,
    cell_out, net_out, full,
    cell, net, grad, w1, w2, cell_pin, net_pin, count,
    code_send, code, tab, net_t, w1_t, hot_cell, hot_net, net_all, grad_all, pre_all, hid_grad_all, pre_grad_all, total,
    own_grad, grad_send, grad_in, net_sum, net_send, net_recv,
    core_send, core_recv, bat_send, bat_recv, part_bat, z_send, z_recv,
    load_sem,
    code_ssem, code_rsem, net_sem, up_ssem, down_ssem, tab_rsem, gsend_sem, grecv_sem, nsum_sem,
    core_ssem, core_rsem, bat_ssem, bat_rsem, z_ssem, z_rsem, gcore_ssem, gcore_rsem, gbat_ssem, gbat_rsem, gz_ssem, gz_rsem,
):
    bat = lax.axis_index("batch")
    me = lax.axis_index("dom")
    cells, feat = cell.shape
    nets = net.shape[0]
    mid = w1.shape[1]
    cap = cell_pin.shape[1]
    core = lax.rem(me, 2)
    z = me // 2
    sibling = me + 1 - 2 * core
    half = total.shape[0] // 2
    has_up = z < depth - 1
    has_down = z > 0
    at_end = jnp.logical_or(z == 0, z == depth - 1)
    above = (bat, 2 * lax.rem(z + 1, depth) + core)
    below = (bat, 2 * lax.rem(z + depth - 1, depth) + core)
    tab_chunks = tab_rsem.shape[1]
    tab_rows = feat // tab_chunks
    grad_chunks = gsend_sem.shape[1]
    grad_rows = cells // grad_chunks

    loads = [
        pltpu.make_async_copy(a, b, load_sem.at[i])
        for i, (a, b) in enumerate(
            (
                (cell_hbm, cell), (cell_pin_hbm, cell_pin), (net_pin_hbm, net_pin),
                (count_hbm, count), (net_hbm, net), (grad_hbm, grad), (w1_hbm, w1), (w2_hbm, w2),
            )
        )
    ]
    for load in loads:
        load.start()

    barrier = pltpu.get_barrier_semaphore()

    def greet_lane(k, carry):
        pl.semaphore_signal(
            barrier, inc=1, device_id=(bat, 2 * lax.rem(z + k, depth) + core), device_id_type=MESH
        )
        return carry

    def greet_batch(k, carry):
        pl.semaphore_signal(
            barrier, inc=1, device_id=(lax.rem(bat + k, batches), me), device_id_type=MESH
        )
        return carry

    lax.fori_loop(1, depth, greet_lane, 0)
    lax.fori_loop(1, batches, greet_batch, 0)
    pl.semaphore_signal(barrier, inc=1, device_id=(bat, sibling), device_id_type=MESH)

    for load in loads[:4]:
        load.wait()
    tab[z] = cell[...].T
    lane = lax.broadcasted_iota(jnp.int32, (1, cap), 1)

    def make_code(t, carry):
        for i in range(2):
            to = 2 * t + i
            live = lane < count[0, to]
            code_send[t, 0:1, i * cap : (i + 1) * cap] = jnp.where(live, cell_pin[pl.ds(to, 1), :], -1)
            code_send[t, 1:2, i * cap : (i + 1) * cap] = jnp.where(live, net_pin[pl.ds(to, 1), :], -1)
        return carry

    lax.fori_loop(0, depth, make_code, 0)
    code[z] = code_send[z]
    for load in loads[4:]:
        load.wait()
    net_t[core, 0:feat, :] = net[...].T
    net_t[core, feat:, :] = grad[...].T
    w1_t[...] = w1[...].T

    pl.semaphore_wait(barrier, depth + batches - 1)

    def code_copy(to, frm):
        return pltpu.make_async_remote_copy(
            src_ref=code_send.at[to], dst_ref=code.at[frm],
            send_sem=code_ssem.at[to], recv_sem=code_rsem.at[frm],
            device_id=(bat, 2 * to + core), device_id_type=MESH,
        )

    def net_copy(side):
        return pltpu.make_async_remote_copy(
            src_ref=net_t.at[side], dst_ref=net_t.at[side],
            send_sem=net_sem.at[0], recv_sem=net_sem.at[1],
            device_id=(bat, sibling), device_id_type=MESH,
        )

    def tab_copy(t, c, upward):
        rows = pl.ds(c * tab_rows, tab_rows)
        return pltpu.make_async_remote_copy(
            src_ref=tab.at[t, rows, :], dst_ref=tab.at[t, rows, :],
            send_sem=(up_ssem if upward else down_ssem).at[t, c], recv_sem=tab_rsem.at[t, c],
            device_id=above if upward else below, device_id_type=MESH,
        )

    def grad_copy(t, c, upward):
        rows, slot = pl.ds(c * grad_rows, grad_rows), t + 1 if upward else t
        return pltpu.make_async_remote_copy(
            src_ref=grad_send.at[t, rows, :], dst_ref=grad_in.at[slot, rows, :],
            send_sem=gsend_sem.at[t, c], recv_sem=grecv_sem.at[slot, c],
            device_id=above if upward else below, device_id_type=MESH,
        )

    def send_codes(k, carry):
        code_copy(lax.rem(z + k, depth), z).start()
        return carry

    net_copy(core).start()
    lax.fori_loop(1, depth, send_codes, 0)
    for c in range(tab_chunks):

        @pl.when(has_up)
        def _():
            tab_copy(z, c, True).start()

        @pl.when(has_down)
        def _():
            tab_copy(z, c, False).start()

    total[...] = jnp.zeros_like(total)
    net_sum[...] = jnp.zeros_like(net_sum)
    net_copy(1 - core).wait_recv()

    def early(k, carry):
        t = lax.rem(z + k, depth)

        @pl.when(k > 0)
        def _():
            code_copy(t, t).wait_recv()

        hot_net[t] = one_hot_t(code[t, 1:2, :], nets)
        for i in range(2):
            cols = slice(i * cap, (i + 1) * cap)
            rows = mm(net_t[i], hot_net[t, :, cols]).astype(BF)
            net_all[t, :, cols] = rows[0:feat, :]
            grad_all[t, :, cols] = rows[feat:, :]
        pre_all[t] = mm(w1_t[:, feat:], net_all[t])
        hid_grad_all[t] = mm(w2[...], grad_all[t])
        return carry

    lax.fori_loop(0, depth, early, 0)

    def front(t):
        hot_cell[t] = one_hot_t(code[t, 0:1, :], cells)

        @pl.when(jnp.logical_and(at_end, t != z))
        def _():
            for c in range(tab_chunks):
                tab_copy(t, c, True).wait_recv()

        rows = mm(tab[t], hot_cell[t]).astype(BF)
        pre = pre_all[t] + mm(w1_t[:, 0:feat], rows)
        sig = 0.5 + 0.5 * jnp.tanh(0.5 * pre)
        hidden = (pre * sig).astype(BF)
        pre_grad = (hid_grad_all[t] * sig * (1.0 + pre * (1.0 - sig))).astype(BF)
        pre_grad_all[t] = pre_grad
        total[0:feat, 0:mid] += mm_t(rows, pre_grad)
        total[feat:, 0:mid] += mm_t(net_all[t], pre_grad)
        total[:, mid:] += mm_t(hidden, grad_all[t])

    def back(t):
        moved = mm(w1[0:feat, :], pre_grad_all[t]).astype(BF)
        own_grad[t] = mm_t(hot_cell[t], moved)
        for upward, first in ((True, jnp.logical_and(z == 0, t > z)), (False, jnp.logical_and(z == depth - 1, t < z))):

            @pl.when(first)
            def _():
                grad_send[t] = own_grad[t].astype(grad_send.dtype)
                for c in range(grad_chunks):
                    grad_copy(t, c, upward).start()

    def forward(j, c):
        @pl.when(jnp.logical_and(z - j >= 0, has_up))
        def _():
            tab_copy(z - j, c, True).wait_recv()
            tab_copy(z - j, c, True).start()

        @pl.when(jnp.logical_and(z + j < depth, has_down))
        def _():
            tab_copy(z + j, c, False).wait_recv()
            tab_copy(z + j, c, False).start()

    def step(j, carry):
        k = j - 1
        down_ok = z - k >= 0
        up_ok = jnp.logical_and(k > 0, z + k < depth)
        work = (
            (down_ok, front, z - k), (down_ok, back, z - k), (up_ok, front, z + k), (up_ok, back, z + k),
        )
        for c in range(max(tab_chunks, len(work))):
            if c < tab_chunks:
                forward(j, c)
            if c < len(work):
                ok, fn, t = work[c]
                pl.when(ok)(functools.partial(fn, t))
        return carry

    lax.fori_loop(1, depth, step, 0)

    @pl.when(at_end)
    def _():
        front(depth - 1 - z)

    rows_b = part_bat.shape[0]

    def own_rows(side, piece):
        start = pl.multiple_of(side * half + piece * rows_b, rows_b)
        return total[pl.ds(start, rows_b), :]

    def core_copy(piece):
        return pltpu.make_async_remote_copy(
            src_ref=core_send.at[piece], dst_ref=core_recv.at[piece],
            send_sem=core_ssem.at[piece], recv_sem=core_rsem.at[piece],
            device_id=(bat, sibling), device_id_type=MESH,
        )

    def core_go(k, carry):
        piece = lax.rem(bat + k, batches)
        core_send[piece] = own_rows(1 - core, piece).astype(BF)
        core_copy(piece).start()
        return carry

    lax.fori_loop(1, batches + 1, core_go, 0)

    @pl.when(at_end)
    def _():
        back(depth - 1 - z)

    def bat_copy(to, frm):
        return pltpu.make_async_remote_copy(
            src_ref=bat_send.at[to], dst_ref=bat_recv.at[frm],
            send_sem=bat_ssem.at[to], recv_sem=bat_rsem.at[frm],
            device_id=(to, me), device_id_type=MESH,
        )

    def bat_go(k, carry):
        to = lax.rem(bat + k, batches)
        core_copy(to).wait_recv()
        bat_send[to] = (own_rows(core, to) + core_recv[to].astype(F32)).astype(BF)
        bat_copy(to, bat).start()
        return carry

    lax.fori_loop(1, batches, bat_go, 0)
    core_copy(bat).wait_recv()
    part_bat[...] = own_rows(core, bat) + core_recv[bat].astype(F32)

    def net_side(t, carry):
        moved = mm(w1[feat:, :], pre_grad_all[t]).astype(BF)
        for i in range(2):
            cols = slice(i * cap, (i + 1) * cap)
            net_sum[i] += mm_t(hot_net[t, :, cols], moved[:, cols])
        return carry

    lax.fori_loop(0, depth, net_side, 0)

    nsum_copy = pltpu.make_async_remote_copy(
        src_ref=net_send, dst_ref=net_recv, send_sem=nsum_sem.at[0], recv_sem=nsum_sem.at[1],
        device_id=(bat, sibling), device_id_type=MESH,
    )
    net_send[...] = net_sum[1 - core].astype(BF)
    nsum_copy.start()

    def add_and_pass(t, c, upward):
        rows = pl.ds(c * grad_rows, grad_rows)
        grad_copy(t, c, upward).wait_recv()
        came = grad_in[t + 1 if upward else t, rows, :]
        grad_send[t, rows, :] = (own_grad[t, rows, :] + came.astype(F32)).astype(grad_send.dtype)
        grad_copy(t, c, upward).start()

    def pass_on(m, carry):
        up_t = m
        down_t = depth - 1 - m
        for c in range(grad_chunks):

            @pl.when(jnp.logical_and(z > 0, up_t > z))
            def _():
                add_and_pass(up_t, c, True)

            @pl.when(jnp.logical_and(z < depth - 1, down_t < z))
            def _():
                add_and_pass(down_t, c, False)

        return carry

    lax.fori_loop(1, depth - 1, pass_on, 0)

    def bat_add(k, carry):
        frm = lax.rem(bat - k + batches, batches)
        bat_copy(frm, frm).wait_recv()
        part_bat[...] += bat_recv[frm].astype(F32)
        return carry

    lax.fori_loop(1, batches, bat_add, 0)
    split_z = z_send.shape[0] > 1
    z_send[...] = part_bat[...].astype(BF).reshape(z_send.shape)

    def z_copy(to, frm):
        return pltpu.make_async_remote_copy(
            src_ref=z_send.at[to if split_z else 0], dst_ref=z_recv.at[frm],
            send_sem=z_ssem.at[to], recv_sem=z_rsem.at[frm],
            device_id=(bat, 2 * to + core), device_id_type=MESH,
        )

    def z_go(k, carry):
        z_copy(lax.rem(z + k, depth), z).start()
        return carry

    lax.fori_loop(1, depth, z_go, 0)
    z_recv[z] = z_send[z if split_z else 0]

    pass_on(depth - 1, 0)

    def z_wait(k, carry):
        frm = lax.rem(z - k + depth, depth)
        z_copy(frm, frm).wait_recv()
        return carry

    lax.fori_loop(1, depth, z_wait, 0)
    summed = z_recv[0].astype(F32)
    for other in range(1, depth):
        summed += z_recv[other].astype(F32)
    summed = summed.astype(BF)

    def gz_copy(to, frm):
        spot = full.at[core, bat, pl.ds(frm * rows_z, rows_z), :]
        return pltpu.make_async_remote_copy(
            src_ref=spot, dst_ref=spot,
            send_sem=gz_ssem.at[to], recv_sem=gz_rsem.at[frm],
            device_id=(bat, 2 * to + core), device_id_type=MESH,
        )

    def gz_go(k, carry):
        gz_copy(lax.rem(z + k, depth), z).start()
        return carry

    def gz_wait(k, carry):
        frm = lax.rem(z - k + depth, depth)
        gz_copy(frm, frm).wait_recv()
        return carry

    if split_z:
        full[core, bat, pl.ds(pl.multiple_of(z * rows_z, rows_z), rows_z), :] = summed
        lax.fori_loop(1, depth, gz_go, 0)
        lax.fori_loop(1, depth, gz_wait, 0)
    else:
        full[core, bat] = summed

    def gbat_copy(to, frm):
        return pltpu.make_async_remote_copy(
            src_ref=full.at[core, frm], dst_ref=full.at[core, frm],
            send_sem=gbat_ssem.at[to], recv_sem=gbat_rsem.at[frm],
            device_id=(to, me), device_id_type=MESH,
        )

    def gbat_go(k, carry):
        gbat_copy(lax.rem(bat + k, batches), bat).start()
        return carry

    def gcore_copy(side, piece):
        return pltpu.make_async_remote_copy(
            src_ref=full.at[side, piece], dst_ref=full.at[side, piece],
            send_sem=gcore_ssem.at[piece], recv_sem=gcore_rsem.at[piece],
            device_id=(bat, sibling), device_id_type=MESH,
        )

    def gbat_wait(k, carry):
        frm = lax.rem(bat - k + batches, batches)
        gbat_copy(frm, frm).wait_recv()
        gcore_copy(core, frm).start()
        return carry

    lax.fori_loop(1, batches, gbat_go, 0)
    gcore_copy(core, bat).start()

    nsum_copy.wait_recv()
    net_out[...] = net_sum[core] + net_recv[...].astype(F32)
    cell_out[...] = own_grad[z]

    @pl.when(has_down)
    def _():
        for c in range(grad_chunks):
            grad_copy(z, c, True).wait_recv()
        cell_out[...] += grad_in[z + 1].astype(F32)

    @pl.when(has_up)
    def _():
        for c in range(grad_chunks):
            grad_copy(z, c, False).wait_recv()
        cell_out[...] += grad_in[z].astype(F32)

    lax.fori_loop(1, batches, gbat_wait, 0)

    def gcore_wait(piece, carry):
        gcore_copy(1 - core, piece).wait_recv()
        return carry

    lax.fori_loop(0, batches, gcore_wait, 0)

    net_copy(core).wait_send()
    nsum_copy.wait_send()

    def drain_tab(t, carry):
        for c in range(tab_chunks):

            @pl.when(jnp.logical_and(t <= z, has_up))
            def _():
                tab_copy(t, c, True).wait_send()

            @pl.when(jnp.logical_and(t >= z, has_down))
            def _():
                tab_copy(t, c, False).wait_send()

        for c in range(grad_chunks):

            @pl.when(t != z)
            def _():
                grad_copy(t, c, True).wait_send()

        return carry

    lax.fori_loop(0, depth, drain_tab, 0)

    def drain_batch(k, carry):
        to = lax.rem(bat + k, batches)
        bat_copy(to, bat).wait_send()
        gbat_copy(to, bat).wait_send()
        return carry

    def drain_z(k, carry):
        to = lax.rem(z + k, depth)
        code_copy(to, z).wait_send()
        z_copy(to, z).wait_send()
        if split_z:
            gz_copy(to, z).wait_send()
        return carry

    lax.fori_loop(1, batches, drain_batch, 0)
    lax.fori_loop(1, depth, drain_z, 0)

    def drain_core(piece, carry):
        core_copy(piece).wait_send()
        gcore_copy(core, piece).wait_send()
        return carry

    lax.fori_loop(0, batches, drain_core, 0)


def finish(scale, cell_sum, net_sum, full, cell_out, net_out, first, second):
    mid = first.shape[1]
    cell_out[...] = cell_sum[...]
    net_out[...] = net_sum[...]
    first[...] = full[:, 0:mid].astype(F32) * scale
    second[...] = full[:, mid:].astype(F32) * scale


def on_device(cell_feat, net_feat, net_grad, w_first, w_second, pin_cell, pin_net, pin_count):
    owners = lax.axis_size("dom")
    batches = lax.axis_size("batch")
    cell, net, grad = cell_feat[0], net_feat[0], net_grad[0]
    capacity = pin_cell.shape[3]
    cells, feat = cell.shape
    nets = net.shape[0]
    fan_in, mid = w_first.shape
    width = mid + feat
    depth = owners // 2
    scale = 1.0 / math.sqrt(batches * owners * owners * capacity)
    half = fan_in // 2
    rows_b = half // batches
    split_z = rows_b // depth >= 16
    rows_z = rows_b // depth if split_z else rows_b
    parts_z = depth if split_z else 1
    slots = 2 * capacity
    wire = BF if depth <= 4 else F32
    dma = pltpu.SemaphoreType.DMA
    vmem = pltpu.VMEM
    hbm = pl.BlockSpec(memory_space=pltpu.HBM)
    on_chip = pl.BlockSpec(memory_space=pltpu.VMEM)

    def block(rows, columns):
        return pl.BlockSpec((rows // 2, columns), lambda i: (i, 0))

    cell_sum, net_sum, full = pl.pallas_call(
        functools.partial(kernel, batches, depth, rows_z),
        out_shape=(
            jax.ShapeDtypeStruct((cells, feat), F32),
            jax.ShapeDtypeStruct((nets, feat), F32),
            jax.ShapeDtypeStruct((2, batches, rows_b, width), BF),
        ),
        in_specs=[hbm] * 8,
        out_specs=[on_chip] * 3,
        scratch_shapes=[
            vmem((cells, feat), BF),
            vmem((nets, feat), BF),
            vmem((nets, feat), BF),
            vmem((fan_in, mid), BF),
            vmem((mid, feat), BF),
            vmem((owners, capacity), jnp.int32),
            vmem((owners, capacity), jnp.int32),
            pltpu.SMEM((1, owners), jnp.int32),
            vmem((depth, 2, slots), jnp.int32),
            vmem((depth, 2, slots), jnp.int32),
            vmem((depth, feat, cells), BF),
            vmem((2, 2 * feat, nets), BF),
            vmem((mid, fan_in), BF),
            vmem((depth, cells, slots), BF),
            vmem((depth, nets, slots), BF),
            vmem((depth, feat, slots), BF),
            vmem((depth, feat, slots), BF),
            vmem((depth, mid, slots), F32),
            vmem((depth, mid, slots), F32),
            vmem((depth, mid, slots), BF),
            vmem((fan_in, width), F32),
            vmem((depth, cells, feat), F32),
            vmem((depth, cells, feat), wire),
            vmem((depth + 1, cells, feat), wire),
            vmem((2, nets, feat), F32),
            vmem((nets, feat), BF),
            vmem((nets, feat), BF),
            vmem((batches, rows_b, width), BF),
            vmem((batches, rows_b, width), BF),
            vmem((batches, rows_b, width), BF),
            vmem((batches, rows_b, width), BF),
            vmem((rows_b, width), F32),
            vmem((parts_z, rows_z, width), BF),
            vmem((depth, rows_z, width), BF),
            dma((8,)),
            dma((depth,)), dma((depth,)), dma((2,)),
            dma((depth, TAB_CHUNKS)), dma((depth, TAB_CHUNKS)), dma((depth, TAB_CHUNKS)),
            dma((depth, GRAD_CHUNKS)), dma((depth + 1, GRAD_CHUNKS)), dma((2,)),
            dma((batches,)), dma((batches,)), dma((batches,)), dma((batches,)), dma((depth,)), dma((depth,)),
            dma((batches,)), dma((batches,)), dma((batches,)), dma((batches,)), dma((depth,)), dma((depth,)),
        ],
        compiler_params=pltpu.CompilerParams(
            collective_id=0, has_side_effects=True, vmem_limit_bytes=60 * 1024 * 1024
        ),
    )(cell, net, grad, w_first, w_second, pin_cell[0, 0], pin_net[0, 0], pin_count[0])
    cell_out, net_out, first, second = pl.pallas_call(
        functools.partial(finish, scale),
        out_shape=(
            jax.ShapeDtypeStruct((cells, feat), F32),
            jax.ShapeDtypeStruct((nets, feat), F32),
            jax.ShapeDtypeStruct((fan_in, mid), F32),
            jax.ShapeDtypeStruct((mid, feat), F32),
        ),
        grid=(2,),
        in_specs=[block(cells, feat), block(nets, feat), block(fan_in, width)],
        out_specs=[block(cells, feat), block(nets, feat), block(fan_in, mid), block(mid, feat)],
    )(cell_sum, net_sum, full.reshape(fan_in, width))
    return (cell_out[None], net_out[None], first, second)


def solution(mesh):
    return jax.shard_map(
        on_device,
        mesh=mesh,
        in_specs=(
            P("batch", "dom", None),
            P("batch", "dom", None),
            P("batch", "dom", None),
            P(),
            P(),
            P("batch", "dom", None, None),
            P("batch", "dom", None, None),
            P("batch", "dom", None),
        ),
        out_specs=(P("batch", "dom", None), P("batch", "dom", None), P(), P()),
        check_vma=False,
    )
```

```python
import functools
import math

import jax
import jax.numpy as jnp
from jax import lax
from jax.experimental import pallas as pl
from jax.experimental.pallas import tpu as pltpu
from jax.sharding import PartitionSpec as P

BF = jnp.bfloat16
F32 = jnp.float32
MESH = pl.DeviceIdType.MESH
TAB_CHUNKS = 4
GRAD_CHUNKS = 4
LAG = 2


def mm(a, b):
    return jnp.dot(a, b, preferred_element_type=F32)


def mm_t(a, b):
    return lax.dot_general(a, b, (((1,), (1,)), ((), ())), preferred_element_type=F32)


def one_hot_t(row, count):
    at = lax.broadcasted_iota(jnp.int32, (count, row.shape[1]), 0)
    return jnp.where(at == row, 1.0, 0.0).astype(BF)


def kernel(
    batches, depth, rows_z,
    cell_hbm, net_hbm, grad_hbm, w1_hbm, w2_hbm, cell_pin_hbm, net_pin_hbm, count_hbm,
    cell_out, net_out, full,
    cell, net, grad, w1, w2, cell_pin, net_pin, count,
    code_send, code, tab, net_t, w1_t, hot_cell, hot_net, net_all, grad_all, pre_all, hid_grad_all, pre_grad_all, total,
    own_grad, grad_send, grad_in, net_sum, net_send, net_recv,
    core_send, core_recv, bat_send, bat_recv, part_bat, z_send, z_recv,
    load_sem,
    code_ssem, code_rsem, net_sem, up_ssem, down_ssem, tab_rsem, gsend_sem, grecv_sem, nsum_sem,
    core_ssem, core_rsem, bat_ssem, bat_rsem, z_ssem, z_rsem, gcore_ssem, gcore_rsem, gbat_ssem, gbat_rsem, gz_ssem, gz_rsem,
):
    bat = lax.axis_index("batch")
    me = lax.axis_index("dom")
    cells, feat = cell.shape
    nets = net.shape[0]
    mid = w1.shape[1]
    cap = cell_pin.shape[1]
    core = lax.rem(me, 2)
    z = me // 2
    sibling = me + 1 - 2 * core
    half = total.shape[0] // 2
    has_up = z < depth - 1
    has_down = z > 0
    at_end = jnp.logical_or(z == 0, z == depth - 1)
    above = (bat, 2 * lax.rem(z + 1, depth) + core)
    below = (bat, 2 * lax.rem(z + depth - 1, depth) + core)
    tab_chunks = tab_rsem.shape[1]
    tab_rows = feat // tab_chunks
    grad_chunks = gsend_sem.shape[1]
    grad_rows = cells // grad_chunks

    loads = [
        pltpu.make_async_copy(a, b, load_sem.at[i])
        for i, (a, b) in enumerate(
            (
                (cell_hbm, cell), (cell_pin_hbm, cell_pin), (net_pin_hbm, net_pin),
                (count_hbm, count), (net_hbm, net), (grad_hbm, grad), (w1_hbm, w1), (w2_hbm, w2),
            )
        )
    ]
    for load in loads:
        load.start()

    barrier = pltpu.get_barrier_semaphore()

    def greet_lane(k, carry):
        pl.semaphore_signal(
            barrier, inc=1, device_id=(bat, 2 * lax.rem(z + k, depth) + core), device_id_type=MESH
        )
        return carry

    def greet_batch(k, carry):
        pl.semaphore_signal(
            barrier, inc=1, device_id=(lax.rem(bat + k, batches), me), device_id_type=MESH
        )
        return carry

    lax.fori_loop(1, depth, greet_lane, 0)
    lax.fori_loop(1, batches, greet_batch, 0)
    pl.semaphore_signal(barrier, inc=1, device_id=(bat, sibling), device_id_type=MESH)

    for load in loads[:4]:
        load.wait()
    tab[z] = cell[...].T
    lane = lax.broadcasted_iota(jnp.int32, (1, cap), 1)

    def make_code(t, carry):
        for i in range(2):
            to = 2 * t + i
            live = lane < count[0, to]
            code_send[t, 0:1, i * cap : (i + 1) * cap] = jnp.where(live, cell_pin[pl.ds(to, 1), :], -1)
            code_send[t, 1:2, i * cap : (i + 1) * cap] = jnp.where(live, net_pin[pl.ds(to, 1), :], -1)
        return carry

    lax.fori_loop(0, depth, make_code, 0)
    code[z] = code_send[z]
    for load in loads[4:]:
        load.wait()
    net_t[core, 0:feat, :] = net[...].T
    net_t[core, feat:, :] = grad[...].T
    w1_t[...] = w1[...].T

    pl.semaphore_wait(barrier, depth + batches - 1)

    def code_copy(to, frm):
        return pltpu.make_async_remote_copy(
            src_ref=code_send.at[to], dst_ref=code.at[frm],
            send_sem=code_ssem.at[to], recv_sem=code_rsem.at[frm],
            device_id=(bat, 2 * to + core), device_id_type=MESH,
        )

    def net_copy(side):
        return pltpu.make_async_remote_copy(
            src_ref=net_t.at[side], dst_ref=net_t.at[side],
            send_sem=net_sem.at[0], recv_sem=net_sem.at[1],
            device_id=(bat, sibling), device_id_type=MESH,
        )

    def tab_copy(t, c, upward):
        rows = pl.ds(c * tab_rows, tab_rows)
        return pltpu.make_async_remote_copy(
            src_ref=tab.at[t, rows, :], dst_ref=tab.at[t, rows, :],
            send_sem=(up_ssem if upward else down_ssem).at[t, c], recv_sem=tab_rsem.at[t, c],
            device_id=above if upward else below, device_id_type=MESH,
        )

    def grad_copy(t, c, upward):
        rows, slot = pl.ds(c * grad_rows, grad_rows), t + 1 if upward else t
        return pltpu.make_async_remote_copy(
            src_ref=grad_send.at[t, rows, :], dst_ref=grad_in.at[slot, rows, :],
            send_sem=gsend_sem.at[t, c], recv_sem=grecv_sem.at[slot, c],
            device_id=above if upward else below, device_id_type=MESH,
        )

    def send_codes(k, carry):
        code_copy(lax.rem(z + k, depth), z).start()
        return carry

    net_copy(core).start()
    lax.fori_loop(1, depth, send_codes, 0)
    for c in range(tab_chunks):

        @pl.when(has_up)
        def _():
            tab_copy(z, c, True).start()

        @pl.when(has_down)
        def _():
            tab_copy(z, c, False).start()

    total[...] = jnp.zeros_like(total)
    net_sum[...] = jnp.zeros_like(net_sum)
    net_copy(1 - core).wait_recv()

    def early(k, carry):
        t = lax.rem(z + k, depth)

        @pl.when(k > 0)
        def _():
            code_copy(t, t).wait_recv()

        hot_net[t] = one_hot_t(code[t, 1:2, :], nets)
        for i in range(2):
            cols = slice(i * cap, (i + 1) * cap)
            rows = mm(net_t[i], hot_net[t, :, cols]).astype(BF)
            net_all[t, :, cols] = rows[0:feat, :]
            grad_all[t, :, cols] = rows[feat:, :]
        pre_all[t] = mm(w1_t[:, feat:], net_all[t])
        hid_grad_all[t] = mm(w2[...], grad_all[t])
        return carry

    lax.fori_loop(0, depth, early, 0)

    def front(t):
        hot_cell[t] = one_hot_t(code[t, 0:1, :], cells)

        @pl.when(jnp.logical_and(at_end, t != z))
        def _():
            for c in range(tab_chunks):
                tab_copy(t, c, True).wait_recv()

        rows = mm(tab[t], hot_cell[t]).astype(BF)
        pre = pre_all[t] + mm(w1_t[:, 0:feat], rows)
        sig = 0.5 + 0.5 * jnp.tanh(0.5 * pre)
        hidden = (pre * sig).astype(BF)
        pre_grad = (hid_grad_all[t] * sig * (1.0 + pre * (1.0 - sig))).astype(BF)
        pre_grad_all[t] = pre_grad
        total[0:feat, 0:mid] += mm_t(rows, pre_grad)
        total[feat:, 0:mid] += mm_t(net_all[t], pre_grad)
        total[:, mid:] += mm_t(hidden, grad_all[t])

    def back(t):
        moved = mm(w1[0:feat, :], pre_grad_all[t]).astype(BF)
        own_grad[t] = mm_t(hot_cell[t], moved)
        for upward, first in ((True, jnp.logical_and(z == 0, t > z)), (False, jnp.logical_and(z == depth - 1, t < z))):

            @pl.when(first)
            def _():
                grad_send[t] = own_grad[t].astype(grad_send.dtype)
                for c in range(grad_chunks):
                    grad_copy(t, c, upward).start()

    def forward(j, c):
        @pl.when(jnp.logical_and(z - j >= 0, has_up))
        def _():
            tab_copy(z - j, c, True).wait_recv()
            tab_copy(z - j, c, True).start()

        @pl.when(jnp.logical_and(z + j < depth, has_down))
        def _():
            tab_copy(z + j, c, False).wait_recv()
            tab_copy(z + j, c, False).start()

    def step(j, carry):
        k = j - 1
        down_ok = z - k >= 0
        up_ok = jnp.logical_and(k > 0, z + k < depth)
        work = (
            (down_ok, front, z - k), (down_ok, back, z - k), (up_ok, front, z + k), (up_ok, back, z + k),
        )
        for c in range(max(tab_chunks, len(work))):
            if c < tab_chunks:
                forward(j, c)
            if c < len(work):
                ok, fn, t = work[c]
                pl.when(ok)(functools.partial(fn, t))
        return carry

    lax.fori_loop(1, depth, step, 0)

    @pl.when(at_end)
    def _():
        front(depth - 1 - z)

    rows_b = part_bat.shape[0]

    def own_rows(side, piece):
        start = pl.multiple_of(side * half + piece * rows_b, rows_b)
        return total[pl.ds(start, rows_b), :]

    def core_copy(piece):
        return pltpu.make_async_remote_copy(
            src_ref=core_send.at[piece], dst_ref=core_recv.at[piece],
            send_sem=core_ssem.at[piece], recv_sem=core_rsem.at[piece],
            device_id=(bat, sibling), device_id_type=MESH,
        )

    def core_go(k, carry):
        piece = lax.rem(bat + k, batches)
        core_send[piece] = own_rows(1 - core, piece).astype(BF)
        core_copy(piece).start()
        return carry

    lax.fori_loop(1, batches + 1, core_go, 0)

    @pl.when(at_end)
    def _():
        back(depth - 1 - z)

    def bat_copy(to, frm):
        return pltpu.make_async_remote_copy(
            src_ref=bat_send.at[to], dst_ref=bat_recv.at[frm],
            send_sem=bat_ssem.at[to], recv_sem=bat_rsem.at[frm],
            device_id=(to, me), device_id_type=MESH,
        )

    def bat_go(k, carry):
        to = lax.rem(bat + k, batches)
        core_copy(to).wait_recv()
        bat_send[to] = (own_rows(core, to) + core_recv[to].astype(F32)).astype(BF)
        bat_copy(to, bat).start()
        return carry

    lax.fori_loop(1, batches, bat_go, 0)
    core_copy(bat).wait_recv()
    part_bat[...] = own_rows(core, bat) + core_recv[bat].astype(F32)

    def net_side(t, carry):
        moved = mm(w1[feat:, :], pre_grad_all[t]).astype(BF)
        for i in range(2):
            cols = slice(i * cap, (i + 1) * cap)
            net_sum[i] += mm_t(hot_net[t, :, cols], moved[:, cols])
        return carry

    lax.fori_loop(0, depth, net_side, 0)

    nsum_copy = pltpu.make_async_remote_copy(
        src_ref=net_send, dst_ref=net_recv, send_sem=nsum_sem.at[0], recv_sem=nsum_sem.at[1],
        device_id=(bat, sibling), device_id_type=MESH,
    )
    net_send[...] = net_sum[1 - core].astype(BF)
    nsum_copy.start()

    def add_and_pass(t, c, upward):
        rows = pl.ds(pl.multiple_of(c * grad_rows, grad_rows), grad_rows)
        grad_copy(t, c, upward).wait_recv()
        came = grad_in[t + 1 if upward else t, rows, :]
        grad_send[t, rows, :] = (own_grad[t, rows, :] + came.astype(F32)).astype(grad_send.dtype)
        grad_copy(t, c, upward).start()

    def pass_on(tick, carry):
        at = tick - LAG * z
        t = at // grad_chunks

        @pl.when((z > 0) & (t > z) & (t < depth))
        def _():
            add_and_pass(t, lax.rem(at, grad_chunks), True)

        at_down = tick - LAG * (depth - 1 - z)
        t_down = depth - 1 - at_down // grad_chunks

        @pl.when((z < depth - 1) & (t_down < z) & (t_down >= 0))
        def _():
            add_and_pass(t_down, lax.rem(at_down, grad_chunks), False)

        return carry

    last_ticks = (depth - 1) * grad_chunks + LAG
    lax.fori_loop(LAG + 2 * grad_chunks, last_ticks, pass_on, 0)

    def bat_add(k, carry):
        frm = lax.rem(bat - k + batches, batches)
        bat_copy(frm, frm).wait_recv()
        part_bat[...] += bat_recv[frm].astype(F32)
        return carry

    lax.fori_loop(1, batches, bat_add, 0)
    split_z = z_send.shape[0] > 1
    z_send[...] = part_bat[...].astype(BF).reshape(z_send.shape)

    def z_copy(to, frm):
        return pltpu.make_async_remote_copy(
            src_ref=z_send.at[to if split_z else 0], dst_ref=z_recv.at[frm],
            send_sem=z_ssem.at[to], recv_sem=z_rsem.at[frm],
            device_id=(bat, 2 * to + core), device_id_type=MESH,
        )

    def z_go(k, carry):
        z_copy(lax.rem(z + k, depth), z).start()
        return carry

    lax.fori_loop(1, depth, z_go, 0)
    z_recv[z] = z_send[z if split_z else 0]

    lax.fori_loop(last_ticks, depth * grad_chunks + LAG * (depth - 1), pass_on, 0)

    def z_wait(k, carry):
        frm = lax.rem(z - k + depth, depth)
        z_copy(frm, frm).wait_recv()
        return carry

    lax.fori_loop(1, depth, z_wait, 0)
    summed = z_recv[0].astype(F32)
    for other in range(1, depth):
        summed += z_recv[other].astype(F32)
    summed = summed.astype(BF)

    def gz_copy(to, frm):
        spot = full.at[core, bat, pl.ds(frm * rows_z, rows_z), :]
        return pltpu.make_async_remote_copy(
            src_ref=spot, dst_ref=spot,
            send_sem=gz_ssem.at[to], recv_sem=gz_rsem.at[frm],
            device_id=(bat, 2 * to + core), device_id_type=MESH,
        )

    def gz_go(k, carry):
        gz_copy(lax.rem(z + k, depth), z).start()
        return carry

    def gz_wait(k, carry):
        frm = lax.rem(z - k + depth, depth)
        gz_copy(frm, frm).wait_recv()
        return carry

    if split_z:
        full[core, bat, pl.ds(pl.multiple_of(z * rows_z, rows_z), rows_z), :] = summed
        lax.fori_loop(1, depth, gz_go, 0)
        lax.fori_loop(1, depth, gz_wait, 0)
    else:
        full[core, bat] = summed

    def gbat_copy(to, frm):
        return pltpu.make_async_remote_copy(
            src_ref=full.at[core, frm], dst_ref=full.at[core, frm],
            send_sem=gbat_ssem.at[to], recv_sem=gbat_rsem.at[frm],
            device_id=(to, me), device_id_type=MESH,
        )

    def gbat_go(k, carry):
        gbat_copy(lax.rem(bat + k, batches), bat).start()
        return carry

    def gcore_copy(side, piece):
        return pltpu.make_async_remote_copy(
            src_ref=full.at[side, piece], dst_ref=full.at[side, piece],
            send_sem=gcore_ssem.at[piece], recv_sem=gcore_rsem.at[piece],
            device_id=(bat, sibling), device_id_type=MESH,
        )

    def gbat_wait(k, carry):
        frm = lax.rem(bat - k + batches, batches)
        gbat_copy(frm, frm).wait_recv()
        gcore_copy(core, frm).start()
        return carry

    lax.fori_loop(1, batches, gbat_go, 0)
    gcore_copy(core, bat).start()

    nsum_copy.wait_recv()
    net_out[...] = net_sum[core] + net_recv[...].astype(F32)
    cell_out[...] = own_grad[z]

    @pl.when(has_down)
    def _():
        for c in range(grad_chunks):
            grad_copy(z, c, True).wait_recv()
        cell_out[...] += grad_in[z + 1].astype(F32)

    @pl.when(has_up)
    def _():
        for c in range(grad_chunks):
            grad_copy(z, c, False).wait_recv()
        cell_out[...] += grad_in[z].astype(F32)

    lax.fori_loop(1, batches, gbat_wait, 0)

    def gcore_wait(piece, carry):
        gcore_copy(1 - core, piece).wait_recv()
        return carry

    lax.fori_loop(0, batches, gcore_wait, 0)

    net_copy(core).wait_send()
    nsum_copy.wait_send()

    def drain_tab(t, carry):
        for c in range(tab_chunks):

            @pl.when(jnp.logical_and(t <= z, has_up))
            def _():
                tab_copy(t, c, True).wait_send()

            @pl.when(jnp.logical_and(t >= z, has_down))
            def _():
                tab_copy(t, c, False).wait_send()

        for c in range(grad_chunks):

            @pl.when(t != z)
            def _():
                grad_copy(t, c, True).wait_send()

        return carry

    lax.fori_loop(0, depth, drain_tab, 0)

    def drain_batch(k, carry):
        to = lax.rem(bat + k, batches)
        bat_copy(to, bat).wait_send()
        gbat_copy(to, bat).wait_send()
        return carry

    def drain_z(k, carry):
        to = lax.rem(z + k, depth)
        code_copy(to, z).wait_send()
        z_copy(to, z).wait_send()
        if split_z:
            gz_copy(to, z).wait_send()
        return carry

    lax.fori_loop(1, batches, drain_batch, 0)
    lax.fori_loop(1, depth, drain_z, 0)

    def drain_core(piece, carry):
        core_copy(piece).wait_send()
        gcore_copy(core, piece).wait_send()
        return carry

    lax.fori_loop(0, batches, drain_core, 0)


def finish(scale, cell_sum, net_sum, full, cell_out, net_out, first, second):
    mid = first.shape[1]
    cell_out[...] = cell_sum[...]
    net_out[...] = net_sum[...]
    first[...] = full[:, 0:mid].astype(F32) * scale
    second[...] = full[:, mid:].astype(F32) * scale


def on_device(cell_feat, net_feat, net_grad, w_first, w_second, pin_cell, pin_net, pin_count):
    owners = lax.axis_size("dom")
    batches = lax.axis_size("batch")
    cell, net, grad = cell_feat[0], net_feat[0], net_grad[0]
    capacity = pin_cell.shape[3]
    cells, feat = cell.shape
    nets = net.shape[0]
    fan_in, mid = w_first.shape
    width = mid + feat
    depth = owners // 2
    scale = 1.0 / math.sqrt(batches * owners * owners * capacity)
    half = fan_in // 2
    rows_b = half // batches
    split_z = rows_b // depth >= 16
    rows_z = rows_b // depth if split_z else rows_b
    parts_z = depth if split_z else 1
    slots = 2 * capacity
    wire = BF if depth <= 4 else F32
    dma = pltpu.SemaphoreType.DMA
    vmem = pltpu.VMEM
    hbm = pl.BlockSpec(memory_space=pltpu.HBM)
    on_chip = pl.BlockSpec(memory_space=pltpu.VMEM)

    def block(rows, columns):
        return pl.BlockSpec((rows // 2, columns), lambda i: (i, 0))

    cell_sum, net_sum, full = pl.pallas_call(
        functools.partial(kernel, batches, depth, rows_z),
        out_shape=(
            jax.ShapeDtypeStruct((cells, feat), F32),
            jax.ShapeDtypeStruct((nets, feat), F32),
            jax.ShapeDtypeStruct((2, batches, rows_b, width), BF),
        ),
        in_specs=[hbm] * 8,
        out_specs=[on_chip] * 3,
        scratch_shapes=[
            vmem((cells, feat), BF),
            vmem((nets, feat), BF),
            vmem((nets, feat), BF),
            vmem((fan_in, mid), BF),
            vmem((mid, feat), BF),
            vmem((owners, capacity), jnp.int32),
            vmem((owners, capacity), jnp.int32),
            pltpu.SMEM((1, owners), jnp.int32),
            vmem((depth, 2, slots), jnp.int32),
            vmem((depth, 2, slots), jnp.int32),
            vmem((depth, feat, cells), BF),
            vmem((2, 2 * feat, nets), BF),
            vmem((mid, fan_in), BF),
            vmem((depth, cells, slots), BF),
            vmem((depth, nets, slots), BF),
            vmem((depth, feat, slots), BF),
            vmem((depth, feat, slots), BF),
            vmem((depth, mid, slots), F32),
            vmem((depth, mid, slots), F32),
            vmem((depth, mid, slots), BF),
            vmem((fan_in, width), F32),
            vmem((depth, cells, feat), F32),
            vmem((depth, cells, feat), wire),
            vmem((depth + 1, cells, feat), wire),
            vmem((2, nets, feat), F32),
            vmem((nets, feat), BF),
            vmem((nets, feat), BF),
            vmem((batches, rows_b, width), BF),
            vmem((batches, rows_b, width), BF),
            vmem((batches, rows_b, width), BF),
            vmem((batches, rows_b, width), BF),
            vmem((rows_b, width), F32),
            vmem((parts_z, rows_z, width), BF),
            vmem((depth, rows_z, width), BF),
            dma((8,)),
            dma((depth,)), dma((depth,)), dma((2,)),
            dma((depth, TAB_CHUNKS)), dma((depth, TAB_CHUNKS)), dma((depth, TAB_CHUNKS)),
            dma((depth, GRAD_CHUNKS)), dma((depth + 1, GRAD_CHUNKS)), dma((2,)),
            dma((batches,)), dma((batches,)), dma((batches,)), dma((batches,)), dma((depth,)), dma((depth,)),
            dma((batches,)), dma((batches,)), dma((batches,)), dma((batches,)), dma((depth,)), dma((depth,)),
        ],
        compiler_params=pltpu.CompilerParams(
            collective_id=0, has_side_effects=True, vmem_limit_bytes=60 * 1024 * 1024
        ),
    )(cell, net, grad, w_first, w_second, pin_cell[0, 0], pin_net[0, 0], pin_count[0])
    cell_out, net_out, first, second = pl.pallas_call(
        functools.partial(finish, scale),
        out_shape=(
            jax.ShapeDtypeStruct((cells, feat), F32),
            jax.ShapeDtypeStruct((nets, feat), F32),
            jax.ShapeDtypeStruct((fan_in, mid), F32),
            jax.ShapeDtypeStruct((mid, feat), F32),
        ),
        grid=(2,),
        in_specs=[block(cells, feat), block(nets, feat), block(fan_in, width)],
        out_specs=[block(cells, feat), block(nets, feat), block(fan_in, mid), block(mid, feat)],
    )(cell_sum, net_sum, full.reshape(fan_in, width))
    return (cell_out[None], net_out[None], first, second)


def solution(mesh):
    return jax.shard_map(
        on_device,
        mesh=mesh,
        in_specs=(
            P("batch", "dom", None),
            P("batch", "dom", None),
            P("batch", "dom", None),
            P(),
            P(),
            P("batch", "dom", None, None),
            P("batch", "dom", None, None),
            P("batch", "dom", None),
        ),
        out_specs=(P("batch", "dom", None), P("batch", "dom", None), P(), P()),
        check_vma=False,
    )
```

```python
import functools
import math

import jax
import jax.numpy as jnp
from jax import lax
from jax.experimental import pallas as pl
from jax.experimental.pallas import tpu as pltpu
from jax.sharding import PartitionSpec as P

BF = jnp.bfloat16
F32 = jnp.float32
MESH = pl.DeviceIdType.MESH
TAB_CHUNKS = 4
GRAD_CHUNKS = 4
LAG = 2


def mm(a, b):
    return jnp.dot(a, b, preferred_element_type=F32)


def mm_t(a, b):
    return lax.dot_general(a, b, (((1,), (1,)), ((), ())), preferred_element_type=F32)


def one_hot_t(row, count):
    at = lax.broadcasted_iota(jnp.int32, (count, row.shape[1]), 0)
    return jnp.where(at == row, 1.0, 0.0).astype(BF)


def kernel(
    batches, depth, rows_z,
    cell_hbm, net_hbm, grad_hbm, w1_hbm, w2_hbm, cell_pin_hbm, net_pin_hbm, count_hbm,
    cell_out, net_out, full,
    cell, net, grad, w1, w2, cell_pin, net_pin, count,
    code_send, code, tab, net_t, w1_t, hot_cell, hot_net, cell_rows, hidden, net_all, grad_all, pre_all, hid_grad_all,
    pre_grad_all, total,
    own_grad, grad_send, grad_in, net_sum, net_send, net_recv,
    core_send, core_recv, bat_send, bat_recv, part_bat, z_send, z_recv,
    load_sem,
    code_ssem, code_rsem, net_sem, up_ssem, down_ssem, tab_rsem, gsend_sem, grecv_sem, nsum_sem,
    core_ssem, core_rsem, bat_ssem, bat_rsem, z_ssem, z_rsem, gcore_ssem, gcore_rsem, gbat_ssem, gbat_rsem, gz_ssem, gz_rsem,
):
    bat = lax.axis_index("batch")
    me = lax.axis_index("dom")
    cells, feat = cell.shape
    nets = net.shape[0]
    mid = w1.shape[1]
    cap = cell_pin.shape[1]
    core = lax.rem(me, 2)
    z = me // 2
    sibling = me + 1 - 2 * core
    groups, fan_in, wide = total.shape
    half = fan_in // 2
    has_up = z < depth - 1
    has_down = z > 0
    at_end = jnp.logical_or(z == 0, z == depth - 1)
    above = (bat, 2 * lax.rem(z + 1, depth) + core)
    below = (bat, 2 * lax.rem(z + depth - 1, depth) + core)
    tab_chunks = tab_rsem.shape[1]
    tab_rows = feat // tab_chunks
    grad_chunks = gsend_sem.shape[1]
    grad_rows = cells // grad_chunks

    loads = [
        pltpu.make_async_copy(a, b, load_sem.at[i])
        for i, (a, b) in enumerate(
            (
                (cell_hbm, cell), (cell_pin_hbm, cell_pin), (net_pin_hbm, net_pin),
                (count_hbm, count), (net_hbm, net), (grad_hbm, grad), (w1_hbm, w1), (w2_hbm, w2),
            )
        )
    ]
    for load in loads:
        load.start()

    barrier = pltpu.get_barrier_semaphore()

    def greet_lane(k, carry):
        pl.semaphore_signal(
            barrier, inc=1, device_id=(bat, 2 * lax.rem(z + k, depth) + core), device_id_type=MESH
        )
        return carry

    def greet_batch(k, carry):
        pl.semaphore_signal(
            barrier, inc=1, device_id=(lax.rem(bat + k, batches), me), device_id_type=MESH
        )
        return carry

    lax.fori_loop(1, depth, greet_lane, 0)
    lax.fori_loop(1, batches, greet_batch, 0)
    pl.semaphore_signal(barrier, inc=1, device_id=(bat, sibling), device_id_type=MESH)

    for load in loads[:4]:
        load.wait()
    tab[z] = cell[...].T
    lane = lax.broadcasted_iota(jnp.int32, (1, cap), 1)

    def make_code(t, carry):
        for i in range(2):
            to = 2 * t + i
            live = lane < count[0, to]
            code_send[t, 0:1, i * cap : (i + 1) * cap] = jnp.where(live, cell_pin[pl.ds(to, 1), :], -1)
            code_send[t, 1:2, i * cap : (i + 1) * cap] = jnp.where(live, net_pin[pl.ds(to, 1), :], -1)
        return carry

    lax.fori_loop(0, depth, make_code, 0)
    code[z] = code_send[z]
    for load in loads[4:]:
        load.wait()
    net_t[core, 0:feat, :] = net[...].T
    net_t[core, feat:, :] = grad[...].T
    w1_t[...] = w1[...].T

    total[...] = jnp.zeros_like(total)
    net_sum[...] = jnp.zeros_like(net_sum)

    pl.semaphore_wait(barrier, depth + batches - 1)

    def code_copy(to, frm):
        return pltpu.make_async_remote_copy(
            src_ref=code_send.at[to], dst_ref=code.at[frm],
            send_sem=code_ssem.at[to], recv_sem=code_rsem.at[frm],
            device_id=(bat, 2 * to + core), device_id_type=MESH,
        )

    def net_copy(side):
        return pltpu.make_async_remote_copy(
            src_ref=net_t.at[side], dst_ref=net_t.at[side],
            send_sem=net_sem.at[0], recv_sem=net_sem.at[1],
            device_id=(bat, sibling), device_id_type=MESH,
        )

    def tab_copy(t, c, upward):
        rows = pl.ds(c * tab_rows, tab_rows)
        return pltpu.make_async_remote_copy(
            src_ref=tab.at[t, rows, :], dst_ref=tab.at[t, rows, :],
            send_sem=(up_ssem if upward else down_ssem).at[t, c], recv_sem=tab_rsem.at[t, c],
            device_id=above if upward else below, device_id_type=MESH,
        )

    def grad_copy(t, c, upward):
        rows, slot = pl.ds(c * grad_rows, grad_rows), t + 1 if upward else t
        return pltpu.make_async_remote_copy(
            src_ref=grad_send.at[t, rows, :], dst_ref=grad_in.at[slot, rows, :],
            send_sem=gsend_sem.at[t, c], recv_sem=grecv_sem.at[slot, c],
            device_id=above if upward else below, device_id_type=MESH,
        )

    def send_codes(k, carry):
        code_copy(lax.rem(z + k, depth), z).start()
        return carry

    net_copy(core).start()
    lax.fori_loop(1, depth, send_codes, 0)
    for c in range(tab_chunks):

        @pl.when(has_up)
        def _():
            tab_copy(z, c, True).start()

        @pl.when(has_down)
        def _():
            tab_copy(z, c, False).start()

    net_copy(1 - core).wait_recv()

    def early(k, carry):
        t = lax.rem(z + k, depth)

        @pl.when(k > 0)
        def _():
            code_copy(t, t).wait_recv()

        hot_net[t] = one_hot_t(code[t, 1:2, :], nets)
        for i in range(2):
            cols = slice(i * cap, (i + 1) * cap)
            rows = mm(net_t[i], hot_net[t, :, cols]).astype(BF)
            net_all[t, :, cols] = rows[0:feat, :]
            grad_all[t, :, cols] = rows[feat:, :]
        pre_all[t] = mm(w1_t[:, feat:], net_all[t])
        hid_grad_all[t] = mm(w2[...], grad_all[t])
        return carry

    lax.fori_loop(0, depth, early, 0)

    def front(t):
        hot_cell[t] = one_hot_t(code[t, 0:1, :], cells)

        @pl.when(jnp.logical_and(at_end, t != z))
        def _():
            for c in range(tab_chunks):
                tab_copy(t, c, True).wait_recv()

        rows = mm(tab[t], hot_cell[t]).astype(BF)
        cell_rows[...] = rows
        pre = pre_all[t] + mm(w1_t[:, 0:feat], rows)
        sig = 0.5 + 0.5 * jnp.tanh(0.5 * pre)
        hidden[...] = (pre * sig).astype(BF)
        pre_grad_all[t] = (hid_grad_all[t] * sig * (1.0 + pre * (1.0 - sig))).astype(BF)

    def add_total(t, q):
        if q < groups - 1:
            pre_grad = pre_grad_all[t, q * wide : (q + 1) * wide, :]
            total[q, 0:feat, :] += mm_t(cell_rows[...], pre_grad)
            total[q, feat:, :] += mm_t(net_all[t], pre_grad)
        else:
            total[q] += mm_t(hidden[...], grad_all[t])

    def unit(t):
        front(t)
        for q in range(groups):
            add_total(t, q)

    def back(t):
        moved = mm(w1[0:feat, :], pre_grad_all[t]).astype(BF)
        own_grad[t] = mm_t(hot_cell[t], moved)
        for upward, first in ((True, jnp.logical_and(z == 0, t > z)), (False, jnp.logical_and(z == depth - 1, t < z))):

            @pl.when(first)
            def _():
                grad_send[t] = own_grad[t].astype(grad_send.dtype)
                for c in range(grad_chunks):
                    grad_copy(t, c, upward).start()

    def forward(j, c):
        @pl.when(jnp.logical_and(z - j >= 0, has_up))
        def _():
            tab_copy(z - j, c, True).wait_recv()
            tab_copy(z - j, c, True).start()

        @pl.when(jnp.logical_and(z + j < depth, has_down))
        def _():
            tab_copy(z + j, c, False).wait_recv()
            tab_copy(z + j, c, False).start()

    def step(j, carry):
        k = j - 1
        down_ok = z - k >= 0
        up_ok = jnp.logical_and(k > 0, z + k < depth)
        work = (
            (down_ok, unit, z - k), (down_ok, back, z - k), (up_ok, unit, z + k), (up_ok, back, z + k),
        )
        for c in range(max(tab_chunks, len(work))):
            if c < tab_chunks:
                forward(j, c)
            if c < len(work):
                ok, fn, t = work[c]
                pl.when(ok)(functools.partial(fn, t))
        return carry

    lax.fori_loop(1, depth, step, 0)

    rows_b = half // batches
    split_z = z_send.shape[1] > 1
    last = depth - 1 - z

    def own_rows(side, q):
        return total[q, pl.ds(pl.multiple_of(side * half, half), half), :]

    def core_copy(q):
        return pltpu.make_async_remote_copy(
            src_ref=core_send.at[q], dst_ref=core_recv.at[q],
            send_sem=core_ssem.at[q], recv_sem=core_rsem.at[q],
            device_id=(bat, sibling), device_id_type=MESH,
        )

    def core_go(q):
        core_send[q] = own_rows(1 - core, q).astype(BF)
        core_copy(q).start()

    def bat_copy(q, to, frm):
        return pltpu.make_async_remote_copy(
            src_ref=bat_send.at[q, to], dst_ref=bat_recv.at[q, frm],
            send_sem=bat_ssem.at[q, to], recv_sem=bat_rsem.at[q, frm],
            device_id=(to, me), device_id_type=MESH,
        )

    def bat_go(q):
        core_copy(q).wait_recv()
        part = own_rows(core, q) + core_recv[q].astype(F32)
        part_bat[q] = part.reshape(batches, rows_b, wide)
        bat_send[q] = part.astype(BF).reshape(batches, rows_b, wide)

        def go(k, carry):
            bat_copy(q, lax.rem(bat + k, batches), bat).start()
            return carry

        lax.fori_loop(1, batches, go, 0)

    def z_copy(q, to, frm):
        return pltpu.make_async_remote_copy(
            src_ref=z_send.at[q, to if split_z else 0], dst_ref=z_recv.at[q, frm],
            send_sem=z_ssem.at[q, to], recv_sem=z_rsem.at[q, frm],
            device_id=(bat, 2 * to + core), device_id_type=MESH,
        )

    def bat_add(q):
        def add(k, carry):
            frm = lax.rem(bat - k + batches, batches)
            bat_copy(q, frm, frm).wait_recv()
            part_bat[q, bat] += bat_recv[q, frm].astype(F32)
            return carry

        lax.fori_loop(1, batches, add, 0)
        z_send[q] = part_bat[q, bat].astype(BF).reshape(z_send.shape[1:])

        def go(k, carry):
            z_copy(q, lax.rem(z + k, depth), z).start()
            return carry

        lax.fori_loop(1, depth, go, 0)
        z_recv[q, z] = z_send[q, z if split_z else 0]

    def gz_copy(q, to, frm):
        spot = full.at[q, core, bat, pl.ds(frm * rows_z, rows_z), :]
        return pltpu.make_async_remote_copy(
            src_ref=spot, dst_ref=spot,
            send_sem=gz_ssem.at[q, to], recv_sem=gz_rsem.at[q, frm],
            device_id=(bat, 2 * to + core), device_id_type=MESH,
        )

    def z_sum(q):
        def wait(k, carry):
            frm = lax.rem(z - k + depth, depth)
            z_copy(q, frm, frm).wait_recv()
            return carry

        lax.fori_loop(1, depth, wait, 0)
        summed = z_recv[q, 0].astype(F32)
        for other in range(1, depth):
            summed += z_recv[q, other].astype(F32)
        summed = summed.astype(BF)
        if split_z:
            full[q, core, bat, pl.ds(pl.multiple_of(z * rows_z, rows_z), rows_z), :] = summed

            def go(k, carry):
                gz_copy(q, lax.rem(z + k, depth), z).start()
                return carry

            lax.fori_loop(1, depth, go, 0)
        else:
            full[q, core, bat] = summed

    def gbat_copy(q, to, frm):
        return pltpu.make_async_remote_copy(
            src_ref=full.at[q, core, frm], dst_ref=full.at[q, core, frm],
            send_sem=gbat_ssem.at[q, to], recv_sem=gbat_rsem.at[q, frm],
            device_id=(to, me), device_id_type=MESH,
        )

    def gbat_go(q):
        if split_z:

            def wait(k, carry):
                frm = lax.rem(z - k + depth, depth)
                gz_copy(q, frm, frm).wait_recv()
                return carry

            lax.fori_loop(1, depth, wait, 0)

        def go(k, carry):
            gbat_copy(q, lax.rem(bat + k, batches), bat).start()
            return carry

        lax.fori_loop(1, batches, go, 0)

    def gcore_copy(q, side):
        return pltpu.make_async_remote_copy(
            src_ref=full.at[q, side], dst_ref=full.at[q, side],
            send_sem=gcore_ssem.at[q], recv_sem=gcore_rsem.at[q],
            device_id=(bat, sibling), device_id_type=MESH,
        )

    def gcore_go(q):
        def wait(k, carry):
            frm = lax.rem(bat - k + batches, batches)
            gbat_copy(q, frm, frm).wait_recv()
            return carry

        lax.fori_loop(1, batches, wait, 0)
        gcore_copy(q, core).start()

    pl.when(at_end)(functools.partial(front, last))
    for q in range(groups):
        pl.when(at_end)(functools.partial(add_total, last, q))
        core_go(q)
        if q > 0:
            bat_go(q - 1)
    pl.when(at_end)(functools.partial(back, last))
    bat_go(groups - 1)

    def net_side(t, carry):
        moved = mm(w1[feat:, :], pre_grad_all[t]).astype(BF)
        for i in range(2):
            cols = slice(i * cap, (i + 1) * cap)
            net_sum[i] += mm_t(hot_net[t, :, cols], moved[:, cols])
        return carry

    lax.fori_loop(0, depth, net_side, 0)

    nsum_copy = pltpu.make_async_remote_copy(
        src_ref=net_send, dst_ref=net_recv, send_sem=nsum_sem.at[0], recv_sem=nsum_sem.at[1],
        device_id=(bat, sibling), device_id_type=MESH,
    )
    net_send[...] = net_sum[1 - core].astype(BF)
    nsum_copy.start()

    def add_and_pass(t, c, upward):
        rows = pl.ds(pl.multiple_of(c * grad_rows, grad_rows), grad_rows)
        grad_copy(t, c, upward).wait_recv()
        came = grad_in[t + 1 if upward else t, rows, :]
        grad_send[t, rows, :] = (own_grad[t, rows, :] + came.astype(F32)).astype(grad_send.dtype)
        grad_copy(t, c, upward).start()

    def pass_on(tick, carry):
        at = tick - LAG * z
        t = at // grad_chunks

        @pl.when((z > 0) & (t > z) & (t < depth))
        def _():
            add_and_pass(t, lax.rem(at, grad_chunks), True)

        at_down = tick - LAG * (depth - 1 - z)
        t_down = depth - 1 - at_down // grad_chunks

        @pl.when((z < depth - 1) & (t_down < z) & (t_down >= 0))
        def _():
            add_and_pass(t_down, lax.rem(at_down, grad_chunks), False)

        return carry

    first_tick = LAG + 2 * grad_chunks
    last_tick = (depth - 1) * grad_chunks + LAG
    end_tick = depth * grad_chunks + LAG * (depth - 2)
    lax.fori_loop(first_tick, last_tick, pass_on, 0)

    stages = [(bat_add, 2), (z_sum, 3), (gbat_go, 3), (gcore_go, 2)]
    events, at = [], 0
    for s, (stage, _) in enumerate(stages):
        for q in range(groups):
            events.append((2 * q + 3 * s, s, stage, q))
    events.sort(key=lambda event: event[:2])
    tick = last_tick
    for i, (_, _, stage, q) in enumerate(events):
        stage(q)
        upto = last_tick + (end_tick - last_tick) * (i + 1) // len(events)
        if upto > tick:
            lax.fori_loop(tick, upto, pass_on, 0)
            tick = upto

    nsum_copy.wait_recv()
    net_out[...] = net_sum[core] + net_recv[...].astype(F32)
    cell_out[...] = own_grad[z]

    @pl.when(has_down)
    def _():
        for c in range(grad_chunks):
            grad_copy(z, c, True).wait_recv()
        cell_out[...] += grad_in[z + 1].astype(F32)

    @pl.when(has_up)
    def _():
        for c in range(grad_chunks):
            grad_copy(z, c, False).wait_recv()
        cell_out[...] += grad_in[z].astype(F32)

    for q in range(groups):
        gcore_copy(q, 1 - core).wait_recv()

    net_copy(core).wait_send()
    nsum_copy.wait_send()

    def drain_tab(t, carry):
        for c in range(tab_chunks):

            @pl.when(jnp.logical_and(t <= z, has_up))
            def _():
                tab_copy(t, c, True).wait_send()

            @pl.when(jnp.logical_and(t >= z, has_down))
            def _():
                tab_copy(t, c, False).wait_send()

        for c in range(grad_chunks):

            @pl.when(t != z)
            def _():
                grad_copy(t, c, True).wait_send()

        return carry

    lax.fori_loop(0, depth, drain_tab, 0)

    def drain_batch(k, carry):
        to = lax.rem(bat + k, batches)
        for q in range(groups):
            bat_copy(q, to, bat).wait_send()
            gbat_copy(q, to, bat).wait_send()
        return carry

    def drain_z(k, carry):
        to = lax.rem(z + k, depth)
        code_copy(to, z).wait_send()
        for q in range(groups):
            z_copy(q, to, z).wait_send()
            if split_z:
                gz_copy(q, to, z).wait_send()
        return carry

    lax.fori_loop(1, batches, drain_batch, 0)
    lax.fori_loop(1, depth, drain_z, 0)

    for q in range(groups):
        core_copy(q).wait_send()
        gcore_copy(q, core).wait_send()


def finish(scale, cell_sum, net_sum, full, cell_out, net_out, first_out, second_out, first, second, sem):
    groups, rows, wide = full.shape
    copies = [
        pltpu.make_async_copy(cell_sum, cell_out, sem.at[0, 0]), pltpu.make_async_copy(net_sum, net_out, sem.at[0, 1]),
    ]
    for copy in copies:
        copy.start()
    parts = sem.shape[1]
    for i in range(parts):
        part = slice(i * rows // parts, (i + 1) * rows // parts)
        for q in range(groups - 1):
            first[part, q * wide : (q + 1) * wide] = full[q, part, :].astype(F32) * scale
        second[part, :] = full[groups - 1, part, :].astype(F32) * scale
        for j, (a, b) in enumerate(((first, first_out), (second, second_out))):
            copies.append(pltpu.make_async_copy(a.at[part, :], b.at[part, :], sem.at[1 + j, i]))
            copies[-1].start()
    for copy in copies:
        copy.wait()


def on_device(cell_feat, net_feat, net_grad, w_first, w_second, pin_cell, pin_net, pin_count):
    owners = lax.axis_size("dom")
    batches = lax.axis_size("batch")
    cell, net, grad = cell_feat[0], net_feat[0], net_grad[0]
    capacity = pin_cell.shape[3]
    cells, feat = cell.shape
    nets = net.shape[0]
    fan_in, mid = w_first.shape
    groups = mid // feat + 1
    depth = owners // 2
    scale = 1.0 / math.sqrt(batches * owners * owners * capacity)
    half = fan_in // 2
    rows_b = half // batches
    split_z = rows_b // depth >= 16
    rows_z = rows_b // depth if split_z else rows_b
    parts_z = depth if split_z else 1
    slots = 2 * capacity
    wire = BF if depth <= 4 else F32
    dma = pltpu.SemaphoreType.DMA
    vmem = pltpu.VMEM
    hbm = pl.BlockSpec(memory_space=pltpu.HBM)
    on_chip = pl.BlockSpec(memory_space=pltpu.VMEM)

    cell_sum, net_sum, full = pl.pallas_call(
        functools.partial(kernel, batches, depth, rows_z),
        out_shape=(
            vmem((cells, feat), F32),
            vmem((nets, feat), F32),
            vmem((groups, 2, batches, rows_b, feat), BF),
        ),
        in_specs=[hbm] * 8,
        out_specs=[on_chip] * 3,
        scratch_shapes=[
            vmem((cells, feat), BF),
            vmem((nets, feat), BF),
            vmem((nets, feat), BF),
            vmem((fan_in, mid), BF),
            vmem((mid, feat), BF),
            vmem((owners, capacity), jnp.int32),
            vmem((owners, capacity), jnp.int32),
            pltpu.SMEM((1, owners), jnp.int32),
            vmem((depth, 2, slots), jnp.int32),
            vmem((depth, 2, slots), jnp.int32),
            vmem((depth, feat, cells), BF),
            vmem((2, 2 * feat, nets), BF),
            vmem((mid, fan_in), BF),
            vmem((depth, cells, slots), BF),
            vmem((depth, nets, slots), BF),
            vmem((feat, slots), BF),
            vmem((mid, slots), BF),
            vmem((depth, feat, slots), BF),
            vmem((depth, feat, slots), BF),
            vmem((depth, mid, slots), F32),
            vmem((depth, mid, slots), F32),
            vmem((depth, mid, slots), BF),
            vmem((groups, fan_in, feat), F32),
            vmem((depth, cells, feat), F32),
            vmem((depth, cells, feat), wire),
            vmem((depth + 1, cells, feat), wire),
            vmem((2, nets, feat), F32),
            vmem((nets, feat), BF),
            vmem((nets, feat), BF),
            vmem((groups, half, feat), BF),
            vmem((groups, half, feat), BF),
            vmem((groups, batches, rows_b, feat), BF),
            vmem((groups, batches, rows_b, feat), BF),
            vmem((groups, batches, rows_b, feat), F32),
            vmem((groups, parts_z, rows_z, feat), BF),
            vmem((groups, depth, rows_z, feat), BF),
            dma((8,)),
            dma((depth,)), dma((depth,)), dma((2,)),
            dma((depth, TAB_CHUNKS)), dma((depth, TAB_CHUNKS)), dma((depth, TAB_CHUNKS)),
            dma((depth, GRAD_CHUNKS)), dma((depth + 1, GRAD_CHUNKS)), dma((2,)),
            dma((groups,)), dma((groups,)), dma((groups, batches)), dma((groups, batches)),
            dma((groups, depth)), dma((groups, depth)), dma((groups,)), dma((groups,)),
            dma((groups, batches)), dma((groups, batches)), dma((groups, depth)), dma((groups, depth)),
        ],
        compiler_params=pltpu.CompilerParams(
            collective_id=0, has_side_effects=True, vmem_limit_bytes=60 * 1024 * 1024
        ),
    )(cell, net, grad, w_first, w_second, pin_cell[0, 0], pin_net[0, 0], pin_count[0])
    cell_out, net_out, first, second = pl.pallas_call(
        functools.partial(finish, scale),
        out_shape=(
            jax.ShapeDtypeStruct((cells, feat), F32),
            jax.ShapeDtypeStruct((nets, feat), F32),
            jax.ShapeDtypeStruct((fan_in, mid), F32),
            jax.ShapeDtypeStruct((mid, feat), F32),
        ),
        in_specs=[on_chip] * 3,
        out_specs=[hbm] * 4,
        scratch_shapes=[vmem((fan_in, mid), F32), vmem((mid, feat), F32), dma((3, 2))],
    )(*(pltpu.with_memory_space_constraint(x, pltpu.VMEM) for x in (cell_sum, net_sum, full.reshape(groups, fan_in, feat))))
    return (cell_out[None], net_out[None], first, second)


def solution(mesh):
    return jax.shard_map(
        on_device,
        mesh=mesh,
        in_specs=(
            P("batch", "dom", None),
            P("batch", "dom", None),
            P("batch", "dom", None),
            P(),
            P(),
            P("batch", "dom", None, None),
            P("batch", "dom", None, None),
            P("batch", "dom", None),
        ),
        out_specs=(P("batch", "dom", None), P("batch", "dom", None), P(), P()),
        check_vma=False,
    )
```

```python
import functools
import math

import jax
import jax.numpy as jnp
from jax import lax
from jax.experimental import pallas as pl
from jax.experimental.pallas import tpu as pltpu
from jax.sharding import PartitionSpec as P

BF = jnp.bfloat16
F32 = jnp.float32
MESH = pl.DeviceIdType.MESH
TAB_CHUNKS = 4
GRAD_CHUNKS = 4
LAG = 2
QUEUE = 2


def mm(a, b):
    return jnp.dot(a, b, preferred_element_type=F32)


def mm_t(a, b):
    return lax.dot_general(a, b, (((1,), (1,)), ((), ())), preferred_element_type=F32)


def one_hot_t(row, count):
    at = lax.broadcasted_iota(jnp.int32, (count, row.shape[1]), 0)
    return jnp.where(at == row, 1.0, 0.0).astype(BF)


def kernel(
    batches, depth, rows_z,
    cell_hbm, net_hbm, grad_hbm, w1_hbm, w2_hbm, cell_pin_hbm, net_pin_hbm, count_hbm,
    cell_out, net_out, full,
    cell, net, grad, w1, w2, cell_pin, net_pin, count,
    code_send, code, tab, net_t, w1_t, hot_cell, hot_net, cell_rows, hidden, net_all, grad_all, pre_all, hid_grad_all,
    pre_grad_all, total,
    own_grad, grad_send, grad_in, net_sum, net_send, net_recv,
    core_send, core_recv, bat_send, bat_recv, part_bat, z_send, z_recv,
    load_sem,
    code_ssem, code_rsem, net_sem, up_ssem, down_ssem, tab_rsem, gsend_sem, grecv_sem, nsum_sem,
    core_ssem, core_rsem, bat_ssem, bat_rsem, z_ssem, z_rsem, gcore_ssem, gcore_rsem, gbat_ssem, gbat_rsem, gz_ssem, gz_rsem,
):
    bat = lax.axis_index("batch")
    me = lax.axis_index("dom")
    cells, feat = cell.shape
    nets = net.shape[0]
    mid = w1.shape[1]
    cap = cell_pin.shape[1]
    core = lax.rem(me, 2)
    z = me // 2
    sibling = me + 1 - 2 * core
    groups, fan_in, wide = total.shape
    half = fan_in // 2
    has_up = z < depth - 1
    has_down = z > 0
    at_end = jnp.logical_or(z == 0, z == depth - 1)
    above = (bat, 2 * lax.rem(z + 1, depth) + core)
    below = (bat, 2 * lax.rem(z + depth - 1, depth) + core)
    tab_chunks = tab_rsem.shape[1]
    tab_rows = feat // tab_chunks
    grad_chunks = gsend_sem.shape[1]
    grad_rows = cells // grad_chunks

    loads = [
        pltpu.make_async_copy(a, b, load_sem.at[i])
        for i, (a, b) in enumerate(
            (
                (cell_hbm, cell), (cell_pin_hbm, cell_pin), (net_pin_hbm, net_pin),
                (count_hbm, count), (net_hbm, net), (grad_hbm, grad), (w1_hbm, w1), (w2_hbm, w2),
            )
        )
    ]
    for load in loads:
        load.start()

    barrier = pltpu.get_barrier_semaphore()

    def greet_lane(k, carry):
        pl.semaphore_signal(
            barrier, inc=1, device_id=(bat, 2 * lax.rem(z + k, depth) + core), device_id_type=MESH
        )
        return carry

    def greet_batch(k, carry):
        pl.semaphore_signal(
            barrier, inc=1, device_id=(lax.rem(bat + k, batches), me), device_id_type=MESH
        )
        return carry

    lax.fori_loop(1, depth, greet_lane, 0)
    lax.fori_loop(1, batches, greet_batch, 0)
    pl.semaphore_signal(barrier, inc=1, device_id=(bat, sibling), device_id_type=MESH)

    for load in loads[:4]:
        load.wait()
    tab[z] = cell[...].T
    lane = lax.broadcasted_iota(jnp.int32, (1, cap), 1)

    def make_code(t, carry):
        for i in range(2):
            to = 2 * t + i
            live = lane < count[0, to]
            code_send[t, 0:1, i * cap : (i + 1) * cap] = jnp.where(live, cell_pin[pl.ds(to, 1), :], -1)
            code_send[t, 1:2, i * cap : (i + 1) * cap] = jnp.where(live, net_pin[pl.ds(to, 1), :], -1)
        return carry

    lax.fori_loop(0, depth, make_code, 0)
    code[z] = code_send[z]
    for load in loads[4:]:
        load.wait()
    net_t[core, 0:feat, :] = net[...].T
    net_t[core, feat:, :] = grad[...].T
    w1_t[...] = w1[...].T

    total[...] = jnp.zeros_like(total)
    net_sum[...] = jnp.zeros_like(net_sum)

    pl.semaphore_wait(barrier, depth + batches - 1)

    def code_copy(to, frm):
        return pltpu.make_async_remote_copy(
            src_ref=code_send.at[to], dst_ref=code.at[frm],
            send_sem=code_ssem.at[to], recv_sem=code_rsem.at[frm],
            device_id=(bat, 2 * to + core), device_id_type=MESH,
        )

    def net_copy(side):
        return pltpu.make_async_remote_copy(
            src_ref=net_t.at[side], dst_ref=net_t.at[side],
            send_sem=net_sem.at[0], recv_sem=net_sem.at[1],
            device_id=(bat, sibling), device_id_type=MESH,
        )

    def tab_copy(t, c, upward):
        rows = pl.ds(c * tab_rows, tab_rows)
        return pltpu.make_async_remote_copy(
            src_ref=tab.at[t, rows, :], dst_ref=tab.at[t, rows, :],
            send_sem=(up_ssem if upward else down_ssem).at[t, c], recv_sem=tab_rsem.at[t, c],
            device_id=above if upward else below, device_id_type=MESH,
        )

    def grad_copy(t, c, upward):
        rows, slot = pl.ds(c * grad_rows, grad_rows), t + 1 if upward else t
        return pltpu.make_async_remote_copy(
            src_ref=grad_send.at[t, rows, :], dst_ref=grad_in.at[slot, rows, :],
            send_sem=gsend_sem.at[t, c], recv_sem=grecv_sem.at[slot, c],
            device_id=above if upward else below, device_id_type=MESH,
        )

    def send_codes(k, carry):
        code_copy(lax.rem(z + k, depth), z).start()
        return carry

    net_copy(core).start()
    lax.fori_loop(1, depth, send_codes, 0)
    for c in range(tab_chunks):

        @pl.when(has_up)
        def _():
            tab_copy(z, c, True).start()

        @pl.when(has_down)
        def _():
            tab_copy(z, c, False).start()

    net_copy(1 - core).wait_recv()

    def early(k, carry):
        t = lax.rem(z + k, depth)

        @pl.when(k > 0)
        def _():
            code_copy(t, t).wait_recv()

        hot_net[t] = one_hot_t(code[t, 1:2, :], nets)
        for i in range(2):
            cols = slice(i * cap, (i + 1) * cap)
            rows = mm(net_t[i], hot_net[t, :, cols]).astype(BF)
            net_all[t, :, cols] = rows[0:feat, :]
            grad_all[t, :, cols] = rows[feat:, :]
        pre_all[t] = mm(w1_t[:, feat:], net_all[t])
        hid_grad_all[t] = mm(w2[...], grad_all[t])
        return carry

    lax.fori_loop(0, depth, early, 0)

    def front(t):
        hot_cell[t] = one_hot_t(code[t, 0:1, :], cells)

        @pl.when(jnp.logical_and(at_end, t != z))
        def _():
            for c in range(tab_chunks):
                tab_copy(t, c, True).wait_recv()

        rows = mm(tab[t], hot_cell[t]).astype(BF)
        cell_rows[...] = rows
        pre = pre_all[t] + mm(w1_t[:, 0:feat], rows)
        sig = 0.5 + 0.5 * jnp.tanh(0.5 * pre)
        hidden[...] = (pre * sig).astype(BF)
        pre_grad_all[t] = (hid_grad_all[t] * sig * (1.0 + pre * (1.0 - sig))).astype(BF)

    def add_total(t, q):
        if q < groups - 1:
            pre_grad = pre_grad_all[t, q * wide : (q + 1) * wide, :]
            total[q, 0:feat, :] += mm_t(cell_rows[...], pre_grad)
            total[q, feat:, :] += mm_t(net_all[t], pre_grad)
        else:
            total[q] += mm_t(hidden[...], grad_all[t])

    def unit(t):
        front(t)
        for q in range(groups):
            add_total(t, q)

    def back(t, sent=grad_chunks):
        moved = mm(w1[0:feat, :], pre_grad_all[t]).astype(BF)
        own_grad[t] = mm_t(hot_cell[t], moved)

        @pl.when(at_end & (t != z))
        def _():
            grad_send[t] = own_grad[t].astype(grad_send.dtype)
            for c in range(sent):
                end_go(t, c)

    def net_side(t):
        moved = mm(w1[feat:, :], pre_grad_all[t]).astype(BF)
        for i in range(2):
            cols = slice(i * cap, (i + 1) * cap)
            net_sum[i] += mm_t(hot_net[t, :, cols], moved[:, cols])

    def finish_unit(t):
        back(t)
        net_side(t)

    def end_go(t, c):
        for upward, first in ((True, z == 0), (False, z > 0)):

            @pl.when(first)
            def _():
                grad_copy(t, c, upward).start()

    def end_more(t, c):
        @pl.when(at_end)
        def _():
            grad_copy(t, c - QUEUE, True).wait_send()
            end_go(t, c)

    def forward(j, c):
        @pl.when(jnp.logical_and(z - j >= 0, has_up))
        def _():
            tab_copy(z - j, c, True).wait_recv()
            tab_copy(z - j, c, True).start()

        @pl.when(jnp.logical_and(z + j < depth, has_down))
        def _():
            tab_copy(z + j, c, False).wait_recv()
            tab_copy(z + j, c, False).start()

    def step(j, carry):
        k = j - 1
        down_ok = z - k >= 0
        up_ok = jnp.logical_and(k > 0, z + k < depth)
        work = (
            (down_ok, unit, z - k), (down_ok, finish_unit, z - k), (up_ok, unit, z + k), (up_ok, finish_unit, z + k),
        )
        for c in range(max(tab_chunks, len(work))):
            if c < tab_chunks:
                forward(j, c)
            if c < len(work):
                ok, fn, t = work[c]
                pl.when(ok)(functools.partial(fn, t))
        return carry

    lax.fori_loop(1, depth, step, 0)

    rows_b = half // batches
    last = depth - 1 - z

    def own_rows(side, q):
        return total[q, pl.ds(pl.multiple_of(side * half, half), half), :]

    def core_copy(q):
        return pltpu.make_async_remote_copy(
            src_ref=core_send.at[q], dst_ref=core_recv.at[q],
            send_sem=core_ssem.at[q], recv_sem=core_rsem.at[q],
            device_id=(bat, sibling), device_id_type=MESH,
        )

    def core_go(q):
        core_send[q] = own_rows(1 - core, q).astype(BF)
        core_copy(q).start()

    def bat_copy(q, to, frm):
        return pltpu.make_async_remote_copy(
            src_ref=bat_send.at[q, to], dst_ref=bat_recv.at[q, frm],
            send_sem=bat_ssem.at[q, to], recv_sem=bat_rsem.at[q, frm],
            device_id=(to, me), device_id_type=MESH,
        )

    def bat_go(q):
        core_copy(q).wait_recv()
        part = own_rows(core, q) + core_recv[q].astype(F32)
        part_bat[q] = part.reshape(batches, rows_b, wide)
        bat_send[q] = part.astype(BF).reshape(batches, rows_b, wide)

        def go(k, carry):
            bat_copy(q, lax.rem(bat + k, batches), bat).start()
            return carry

        lax.fori_loop(1, batches, go, 0, unroll=depth <= 4)

    split_z = rows_z < rows_b

    def z_copy(q, to, frm):
        if split_z:
            src = z_send.at[q, pl.ds(to * rows_z, rows_z), :]
            dst = z_recv.at[q, frm, pl.ds(0, rows_z), :]
        else:
            src, dst = z_send.at[q], z_recv.at[q, frm]
        return pltpu.make_async_remote_copy(
            src_ref=src, dst_ref=dst, send_sem=z_ssem.at[q, to], recv_sem=z_rsem.at[q, frm],
            device_id=(bat, 2 * to + core), device_id_type=MESH,
        )

    def bat_add(q):
        def add(k, carry):
            frm = lax.rem(bat - k + batches, batches)
            bat_copy(q, frm, frm).wait_recv()
            part_bat[q, bat] += bat_recv[q, frm].astype(F32)
            return carry

        lax.fori_loop(1, batches, add, 0, unroll=depth <= 4)
        z_send[q] = part_bat[q, bat].astype(BF)

        def go(k, carry):
            z_copy(q, lax.rem(z + k, depth), z).start()
            return carry

        lax.fori_loop(1, depth, go, 0, unroll=depth <= 4)
        if split_z:
            z_recv[q, z, 0:rows_z, :] = z_send[q, pl.ds(pl.multiple_of(z * rows_z, rows_z), rows_z), :]
        else:
            z_recv[q, z] = z_send[q]

    def gz_copy(q, to, frm):
        spot = full.at[q, core, bat, pl.ds(frm * rows_z, rows_z), :]
        return pltpu.make_async_remote_copy(
            src_ref=spot, dst_ref=spot,
            send_sem=gz_ssem.at[q, to], recv_sem=gz_rsem.at[q, frm],
            device_id=(bat, 2 * to + core), device_id_type=MESH,
        )

    def z_sum(q):
        def wait(k, carry):
            frm = lax.rem(z - k + depth, depth)
            z_copy(q, frm, frm).wait_recv()
            return carry

        lax.fori_loop(1, depth, wait, 0, unroll=depth <= 4)
        rows = rows_z if split_z else rows_b
        summed = z_recv[q, 0, 0:rows, :].astype(F32)
        for other in range(1, depth):
            summed += z_recv[q, other, 0:rows, :].astype(F32)
        summed = summed.astype(BF)
        if split_z:
            full[q, core, bat, pl.ds(pl.multiple_of(z * rows_z, rows_z), rows_z), :] = summed

            def go(k, carry):
                gz_copy(q, lax.rem(z + k, depth), z).start()
                return carry

            lax.fori_loop(1, depth, go, 0, unroll=depth <= 4)
        else:
            full[q, core, bat] = summed

    def gbat_copy(q, to, frm):
        return pltpu.make_async_remote_copy(
            src_ref=full.at[q, core, frm], dst_ref=full.at[q, core, frm],
            send_sem=gbat_ssem.at[q, to], recv_sem=gbat_rsem.at[q, frm],
            device_id=(to, me), device_id_type=MESH,
        )

    def gbat_go(q):
        if split_z:

            def wait(k, carry):
                frm = lax.rem(z - k + depth, depth)
                gz_copy(q, frm, frm).wait_recv()
                return carry

            lax.fori_loop(1, depth, wait, 0, unroll=depth <= 4)

        def go(k, carry):
            gbat_copy(q, lax.rem(bat + k, batches), bat).start()
            return carry

        lax.fori_loop(1, batches, go, 0, unroll=depth <= 4)

    def gcore_copy(q, side):
        return pltpu.make_async_remote_copy(
            src_ref=full.at[q, side], dst_ref=full.at[q, side],
            send_sem=gcore_ssem.at[q], recv_sem=gcore_rsem.at[q],
            device_id=(bat, sibling), device_id_type=MESH,
        )

    def gcore_go(q):
        def wait(k, carry):
            frm = lax.rem(bat - k + batches, batches)
            gbat_copy(q, frm, frm).wait_recv()
            return carry

        lax.fori_loop(1, batches, wait, 0, unroll=depth <= 4)
        gcore_copy(q, core).start()

    pl.when(at_end)(functools.partial(front, last))
    for q in range(groups):
        pl.when(at_end)(functools.partial(add_total, last, q))
        core_go(q)
        if q > 0:
            bat_go(q - 1)
    pl.when(at_end)(functools.partial(back, last, QUEUE))
    bat_go(groups - 1)

    pl.when(at_end)(functools.partial(net_side, last))

    nsum_copy = pltpu.make_async_remote_copy(
        src_ref=net_send, dst_ref=net_recv, send_sem=nsum_sem.at[0], recv_sem=nsum_sem.at[1],
        device_id=(bat, sibling), device_id_type=MESH,
    )
    net_send[...] = net_sum[1 - core].astype(BF)
    nsum_copy.start()

    def add_and_pass(t, c, upward):
        rows = pl.ds(pl.multiple_of(c * grad_rows, grad_rows), grad_rows)
        grad_copy(t, c, upward).wait_recv()
        came = grad_in[t + 1 if upward else t, rows, :]
        grad_send[t, rows, :] = (own_grad[t, rows, :] + came.astype(F32)).astype(grad_send.dtype)
        grad_copy(t, c, upward).start()

    def pass_on(tick, carry):
        at = tick - LAG * z
        t = at // grad_chunks

        @pl.when((z > 0) & (t > z) & (t < depth))
        def _():
            add_and_pass(t, lax.rem(at, grad_chunks), True)

        at_down = tick - LAG * (depth - 1 - z)
        t_down = depth - 1 - at_down // grad_chunks

        @pl.when((z < depth - 1) & (t_down < z) & (t_down >= 0))
        def _():
            add_and_pass(t_down, lax.rem(at_down, grad_chunks), False)

        return carry

    first_tick = LAG + 2 * grad_chunks
    last_tick = (depth - 1) * grad_chunks + LAG
    end_tick = depth * grad_chunks + LAG * (depth - 2)
    lax.fori_loop(first_tick, last_tick, pass_on, 0)

    def ticks(frm, to):
        span = end_tick - last_tick
        lax.fori_loop(last_tick + span * frm // 6, last_tick + span * to // 6, pass_on, 0)

    def ticks(part):
        span, parts = end_tick - last_tick, 2 * groups
        lax.fori_loop(last_tick + span * part // parts, last_tick + span * (part + 1) // parts, pass_on, 0)

    for i in range(max(groups, grad_chunks - QUEUE)):
        if i + QUEUE < grad_chunks:
            end_more(last, i + QUEUE)
        if i < groups:
            bat_add(i)
    for q in range(groups):
        ticks(q)
        z_sum(q)
    for q in range(groups):
        gbat_go(q)
        ticks(groups + q)
    for q in range(groups):
        gcore_go(q)

    net_copy(core).wait_send()
    nsum_copy.wait_send()

    def drain_tab(t, carry):
        for c in range(tab_chunks):

            @pl.when(jnp.logical_and(t <= z, has_up))
            def _():
                tab_copy(t, c, True).wait_send()

            @pl.when(jnp.logical_and(t >= z, has_down))
            def _():
                tab_copy(t, c, False).wait_send()

        return carry

    lax.fori_loop(0, depth, drain_tab, 0)

    def drain_batch(k, carry):
        to = lax.rem(bat + k, batches)
        for q in range(groups):
            bat_copy(q, to, bat).wait_send()
        return carry

    def drain_z(k, carry):
        to = lax.rem(z + k, depth)
        code_copy(to, z).wait_send()
        for q in range(groups):
            z_copy(q, to, z).wait_send()
        return carry

    lax.fori_loop(1, batches, drain_batch, 0)
    lax.fori_loop(1, depth, drain_z, 0)
    for q in range(groups):
        core_copy(q).wait_send()

    nsum_copy.wait_recv()
    net_out[...] = net_sum[core] + net_recv[...].astype(F32)
    cell_out[...] = own_grad[z]

    @pl.when(has_down)
    def _():
        for c in range(grad_chunks):
            grad_copy(z, c, True).wait_recv()
        cell_out[...] += grad_in[z + 1].astype(F32)

    @pl.when(has_up)
    def _():
        for c in range(grad_chunks):
            grad_copy(z, c, False).wait_recv()
        cell_out[...] += grad_in[z].astype(F32)

    def drain_grad(t, carry):
        for c in range(grad_chunks):

            @pl.when((t != z) & jnp.logical_not(at_end & (t == last) & (c < grad_chunks - QUEUE)))
            def _():
                grad_copy(t, c, True).wait_send()

        return carry

    lax.fori_loop(0, depth, drain_grad, 0)

    def drain_gbat(k, carry):
        for q in range(groups):
            gbat_copy(q, lax.rem(bat + k, batches), bat).wait_send()
        return carry

    def drain_gz(k, carry):
        for q in range(groups):
            if split_z:
                gz_copy(q, lax.rem(z + k, depth), z).wait_send()
        return carry

    lax.fori_loop(1, batches, drain_gbat, 0)
    lax.fori_loop(1, depth, drain_gz, 0)
    for q in range(groups):
        gcore_copy(q, core).wait_send()

    for q in range(groups):
        gcore_copy(q, 1 - core).wait_recv()


def finish(scale, cell_sum, net_sum, full, cell_out, net_out, first_out, second_out, first, second, sem):
    groups, rows, wide = full.shape
    copies = [
        pltpu.make_async_copy(cell_sum, cell_out, sem.at[0, 0]), pltpu.make_async_copy(net_sum, net_out, sem.at[0, 1]),
    ]
    for copy in copies:
        copy.start()
    parts = sem.shape[1]
    for i in range(parts):
        part = slice(i * rows // parts, (i + 1) * rows // parts)
        for q in range(groups - 1):
            first[part, q * wide : (q + 1) * wide] = full[q, part, :].astype(F32) * scale
        second[part, :] = full[groups - 1, part, :].astype(F32) * scale
        for j, (a, b) in enumerate(((first, first_out), (second, second_out))):
            copies.append(pltpu.make_async_copy(a.at[part, :], b.at[part, :], sem.at[1 + j, i]))
            copies[-1].start()
    for copy in copies:
        copy.wait()


def on_device(cell_feat, net_feat, net_grad, w_first, w_second, pin_cell, pin_net, pin_count):
    owners = lax.axis_size("dom")
    batches = lax.axis_size("batch")
    cell, net, grad = cell_feat[0], net_feat[0], net_grad[0]
    capacity = pin_cell.shape[3]
    cells, feat = cell.shape
    nets = net.shape[0]
    fan_in, mid = w_first.shape
    groups = mid // feat + 1
    depth = owners // 2
    scale = 1.0 / math.sqrt(batches * owners * owners * capacity)
    half = fan_in // 2
    rows_b = half // batches
    split_z = rows_b // depth >= 16
    rows_z = rows_b // depth if split_z else rows_b
    slots = 2 * capacity
    wire = BF if depth <= 4 else F32
    dma = pltpu.SemaphoreType.DMA
    vmem = pltpu.VMEM
    hbm = pl.BlockSpec(memory_space=pltpu.HBM)
    on_chip = pl.BlockSpec(memory_space=pltpu.VMEM)

    cell_sum, net_sum, full = pl.pallas_call(
        functools.partial(kernel, batches, depth, rows_z),
        out_shape=(
            vmem((cells, feat), F32),
            vmem((nets, feat), F32),
            vmem((groups, 2, batches, rows_b, feat), BF),
        ),
        in_specs=[hbm] * 8,
        out_specs=[on_chip] * 3,
        scratch_shapes=[
            vmem((cells, feat), BF),
            vmem((nets, feat), BF),
            vmem((nets, feat), BF),
            vmem((fan_in, mid), BF),
            vmem((mid, feat), BF),
            vmem((owners, capacity), jnp.int32),
            vmem((owners, capacity), jnp.int32),
            pltpu.SMEM((1, owners), jnp.int32),
            vmem((depth, 2, slots), jnp.int32),
            vmem((depth, 2, slots), jnp.int32),
            vmem((depth, feat, cells), BF),
            vmem((2, 2 * feat, nets), BF),
            vmem((mid, fan_in), BF),
            vmem((depth, cells, slots), BF),
            vmem((depth, nets, slots), BF),
            vmem((feat, slots), BF),
            vmem((mid, slots), BF),
            vmem((depth, feat, slots), BF),
            vmem((depth, feat, slots), BF),
            vmem((depth, mid, slots), F32),
            vmem((depth, mid, slots), F32),
            vmem((depth, mid, slots), BF),
            vmem((groups, fan_in, feat), F32),
            vmem((depth, cells, feat), F32),
            vmem((depth, cells, feat), wire),
            vmem((depth + 1, cells, feat), wire),
            vmem((2, nets, feat), F32),
            vmem((nets, feat), BF),
            vmem((nets, feat), BF),
            vmem((groups, half, feat), BF),
            vmem((groups, half, feat), BF),
            vmem((groups, batches, rows_b, feat), BF),
            vmem((groups, batches, rows_b, feat), BF),
            vmem((groups, batches, rows_b, feat), F32),
            vmem((groups, rows_b, feat), BF),
            vmem((groups, depth, rows_b, feat), BF),
            dma((8,)),
            dma((depth,)), dma((depth,)), dma((2,)),
            dma((depth, TAB_CHUNKS)), dma((depth, TAB_CHUNKS)), dma((depth, TAB_CHUNKS)),
            dma((depth, GRAD_CHUNKS)), dma((depth + 1, GRAD_CHUNKS)), dma((2,)),
            dma((groups,)), dma((groups,)), dma((groups, batches)), dma((groups, batches)),
            dma((groups, depth)), dma((groups, depth)), dma((groups,)), dma((groups,)),
            dma((groups, batches)), dma((groups, batches)), dma((groups, depth)), dma((groups, depth)),
        ],
        compiler_params=pltpu.CompilerParams(
            collective_id=0, has_side_effects=True, vmem_limit_bytes=60 * 1024 * 1024
        ),
    )(cell, net, grad, w_first, w_second, pin_cell[0, 0], pin_net[0, 0], pin_count[0])
    cell_out, net_out, first, second = pl.pallas_call(
        functools.partial(finish, scale),
        out_shape=(
            jax.ShapeDtypeStruct((cells, feat), F32),
            jax.ShapeDtypeStruct((nets, feat), F32),
            jax.ShapeDtypeStruct((fan_in, mid), F32),
            jax.ShapeDtypeStruct((mid, feat), F32),
        ),
        in_specs=[on_chip] * 3,
        out_specs=[hbm] * 4,
        scratch_shapes=[vmem((fan_in, mid), F32), vmem((mid, feat), F32), dma((3, 2))],
    )(*(pltpu.with_memory_space_constraint(x, pltpu.VMEM) for x in (cell_sum, net_sum, full.reshape(groups, fan_in, feat))))
    return (cell_out[None], net_out[None], first, second)


def solution(mesh):
    return jax.shard_map(
        on_device,
        mesh=mesh,
        in_specs=(
            P("batch", "dom", None),
            P("batch", "dom", None),
            P("batch", "dom", None),
            P(),
            P(),
            P("batch", "dom", None, None),
            P("batch", "dom", None, None),
            P("batch", "dom", None),
        ),
        out_specs=(P("batch", "dom", None), P("batch", "dom", None), P(), P()),
        check_vma=False,
    )
```

```python
import functools
import math

import jax
import jax.numpy as jnp
from jax import lax
from jax.experimental import pallas as pl
from jax.experimental.pallas import tpu as pltpu
from jax.sharding import PartitionSpec as P

BF = jnp.bfloat16
F32 = jnp.float32
MESH = pl.DeviceIdType.MESH
TAB_CHUNKS = 4
GRAD_CHUNKS = 4
LAG = 2
QUEUE = 2


def mm(a, b):
    return jnp.dot(a, b, preferred_element_type=F32)


def mm_t(a, b):
    return lax.dot_general(a, b, (((1,), (1,)), ((), ())), preferred_element_type=F32)


def one_hot_t(row, count):
    at = lax.broadcasted_iota(jnp.int32, (count, row.shape[1]), 0)
    return jnp.where(at == row, 1.0, 0.0).astype(BF)


def kernel(
    batches, depth, rows_z,
    cell_hbm, net_hbm, grad_hbm, w1_hbm, w2_hbm, cell_pin_hbm, net_pin_hbm, count_hbm,
    cell_out, net_out, full,
    cell, net, grad, w1, w2, cell_pin, net_pin, count,
    code_send, code, tab, net_t, w1_t, hot_cell, hot_net, cell_rows, hidden, net_all, grad_all, pre_all, hid_grad_all,
    pre_grad_all, total,
    own_grad, grad_send, grad_in, net_sum, net_send, net_recv,
    core_send, core_recv, bat_send, bat_recv, part_bat, z_send, z_recv,
    load_sem,
    code_ssem, code_rsem, net_sem, up_ssem, down_ssem, tab_rsem, gsend_sem, grecv_sem, nsum_sem,
    core_ssem, core_rsem, bat_ssem, bat_rsem, z_ssem, z_rsem, gcore_ssem, gcore_rsem, gbat_ssem, gbat_rsem, gz_ssem, gz_rsem,
):
    bat = lax.axis_index("batch")
    me = lax.axis_index("dom")
    cells, feat = cell.shape
    nets = net.shape[0]
    mid = w1.shape[1]
    cap = cell_pin.shape[1]
    core = lax.rem(me, 2)
    z = me // 2
    sibling = me + 1 - 2 * core
    groups, fan_in, wide = total.shape
    half = fan_in // 2
    has_up = z < depth - 1
    has_down = z > 0
    at_end = jnp.logical_or(z == 0, z == depth - 1)
    above = (bat, 2 * lax.rem(z + 1, depth) + core)
    below = (bat, 2 * lax.rem(z + depth - 1, depth) + core)
    tab_chunks = tab_rsem.shape[1]
    tab_rows = feat // tab_chunks
    grad_chunks = gsend_sem.shape[1]
    grad_rows = cells // grad_chunks

    loads = [
        pltpu.make_async_copy(a, b, load_sem.at[i])
        for i, (a, b) in enumerate(
            (
                (cell_hbm, cell), (cell_pin_hbm, cell_pin), (net_pin_hbm, net_pin),
                (count_hbm, count), (net_hbm, net), (grad_hbm, grad), (w1_hbm, w1), (w2_hbm, w2),
            )
        )
    ]
    for load in loads:
        load.start()

    barrier = pltpu.get_barrier_semaphore()

    def greet_lane(k, carry):
        pl.semaphore_signal(
            barrier, inc=1, device_id=(bat, 2 * lax.rem(z + k, depth) + core), device_id_type=MESH
        )
        return carry

    def greet_batch(k, carry):
        pl.semaphore_signal(
            barrier, inc=1, device_id=(lax.rem(bat + k, batches), me), device_id_type=MESH
        )
        return carry

    lax.fori_loop(1, depth, greet_lane, 0)
    lax.fori_loop(1, batches, greet_batch, 0)
    pl.semaphore_signal(barrier, inc=1, device_id=(bat, sibling), device_id_type=MESH)

    for load in loads[:4]:
        load.wait()
    tab[z] = cell[...].T
    lane = lax.broadcasted_iota(jnp.int32, (1, cap), 1)

    def make_code(t, carry):
        for i in range(2):
            to = 2 * t + i
            live = lane < count[0, to]
            code_send[t, 0:1, i * cap : (i + 1) * cap] = jnp.where(live, cell_pin[pl.ds(to, 1), :], -1)
            code_send[t, 1:2, i * cap : (i + 1) * cap] = jnp.where(live, net_pin[pl.ds(to, 1), :], -1)
        return carry

    lax.fori_loop(0, depth, make_code, 0)
    code[z] = code_send[z]
    for load in loads[4:]:
        load.wait()
    net_t[core, 0:feat, :] = net[...].T
    net_t[core, feat:, :] = grad[...].T
    w1_t[...] = w1[...].T

    total[...] = jnp.zeros_like(total)
    net_sum[...] = jnp.zeros_like(net_sum)

    pl.semaphore_wait(barrier, depth + batches - 1)

    def code_copy(to, frm):
        return pltpu.make_async_remote_copy(
            src_ref=code_send.at[to], dst_ref=code.at[frm],
            send_sem=code_ssem.at[to], recv_sem=code_rsem.at[frm],
            device_id=(bat, 2 * to + core), device_id_type=MESH,
        )

    def net_copy(side):
        return pltpu.make_async_remote_copy(
            src_ref=net_t.at[side], dst_ref=net_t.at[side],
            send_sem=net_sem.at[0], recv_sem=net_sem.at[1],
            device_id=(bat, sibling), device_id_type=MESH,
        )

    def tab_copy(t, c, upward):
        rows = pl.ds(c * tab_rows, tab_rows)
        return pltpu.make_async_remote_copy(
            src_ref=tab.at[t, rows, :], dst_ref=tab.at[t, rows, :],
            send_sem=(up_ssem if upward else down_ssem).at[t, c], recv_sem=tab_rsem.at[t, c],
            device_id=above if upward else below, device_id_type=MESH,
        )

    def grad_copy(t, c, upward):
        rows, slot = pl.ds(c * grad_rows, grad_rows), t + 1 if upward else t
        return pltpu.make_async_remote_copy(
            src_ref=grad_send.at[t, rows, :], dst_ref=grad_in.at[slot, rows, :],
            send_sem=gsend_sem.at[t, c], recv_sem=grecv_sem.at[slot, c],
            device_id=above if upward else below, device_id_type=MESH,
        )

    def send_codes(k, carry):
        code_copy(lax.rem(z + k, depth), z).start()
        return carry

    net_copy(core).start()
    lax.fori_loop(1, depth, send_codes, 0)
    for c in range(tab_chunks):

        @pl.when(has_up)
        def _():
            tab_copy(z, c, True).start()

        @pl.when(has_down)
        def _():
            tab_copy(z, c, False).start()

    net_copy(1 - core).wait_recv()

    def early(k, carry):
        t = lax.rem(z + k, depth)

        @pl.when(k > 0)
        def _():
            code_copy(t, t).wait_recv()

        hot_net[t] = one_hot_t(code[t, 1:2, :], nets)
        for i in range(2):
            cols = slice(i * cap, (i + 1) * cap)
            rows = mm(net_t[i], hot_net[t, :, cols]).astype(BF)
            net_all[t, :, cols] = rows[0:feat, :]
            grad_all[t, :, cols] = rows[feat:, :]
        pre_all[t] = mm(w1_t[:, feat:], net_all[t])
        hid_grad_all[t] = mm(w2[...], grad_all[t])
        return carry

    lax.fori_loop(0, depth, early, 0)

    def front(t):
        hot_cell[t] = one_hot_t(code[t, 0:1, :], cells)

        for c in range(tab_chunks):
            part = slice(c * tab_rows, (c + 1) * tab_rows)

            @pl.when(jnp.logical_and(at_end, t != z))
            def _():
                tab_copy(t, c, True).wait_recv()

            cell_rows[part, :] = mm(tab[t, part, :], hot_cell[t]).astype(BF)

        pre = pre_all[t] + mm(w1_t[:, 0:feat], cell_rows[...])
        sig = 0.5 + 0.5 * jnp.tanh(0.5 * pre)
        hidden[...] = (pre * sig).astype(BF)
        pre_grad_all[t] = (hid_grad_all[t] * sig * (1.0 + pre * (1.0 - sig))).astype(BF)

    def add_total(t, q):
        if q < groups - 1:
            pre_grad = pre_grad_all[t, q * wide : (q + 1) * wide, :]
            total[q, 0:feat, :] += mm_t(cell_rows[...], pre_grad)
            total[q, feat:, :] += mm_t(net_all[t], pre_grad)
        else:
            total[q] += mm_t(hidden[...], grad_all[t])

    def unit(t):
        front(t)
        for q in range(groups):
            add_total(t, q)

    def back(t, sent=grad_chunks):
        moved = mm(w1[0:feat, :], pre_grad_all[t]).astype(BF)
        own_grad[t] = mm_t(hot_cell[t], moved)

        @pl.when(at_end & (t != z))
        def _():
            grad_send[t] = own_grad[t].astype(grad_send.dtype)
            for c in range(sent):
                end_go(t, c)

    def net_side(t):
        moved = mm(w1[feat:, :], pre_grad_all[t]).astype(BF)
        for i in range(2):
            cols = slice(i * cap, (i + 1) * cap)
            net_sum[i] += mm_t(hot_net[t, :, cols], moved[:, cols])

    def finish_unit(t):
        back(t)
        net_side(t)

    def end_go(t, c):
        for upward, first in ((True, z == 0), (False, z > 0)):

            @pl.when(first)
            def _():
                grad_copy(t, c, upward).start()

    def end_more(t, c):
        @pl.when(at_end)
        def _():
            grad_copy(t, c - QUEUE, True).wait_send()
            end_go(t, c)

    def forward(j, c):
        @pl.when(jnp.logical_and(z - j >= 0, has_up))
        def _():
            tab_copy(z - j, c, True).wait_recv()
            tab_copy(z - j, c, True).start()

        @pl.when(jnp.logical_and(z + j < depth, has_down))
        def _():
            tab_copy(z + j, c, False).wait_recv()
            tab_copy(z + j, c, False).start()

    def step(j, carry):
        k = j - 1
        down_ok = z - k >= 0
        up_ok = jnp.logical_and(k > 0, z + k < depth)
        work = (
            (down_ok, unit, z - k), (down_ok, finish_unit, z - k), (up_ok, unit, z + k), (up_ok, finish_unit, z + k),
        )
        for c in range(max(tab_chunks, len(work))):
            if c < tab_chunks:
                forward(j, c)
            if c < len(work):
                ok, fn, t = work[c]
                pl.when(ok)(functools.partial(fn, t))
        return carry

    lax.fori_loop(1, depth, step, 0)

    rows_b = half // batches
    last = depth - 1 - z

    def own_rows(side, q):
        return total[q, pl.ds(pl.multiple_of(side * half, half), half), :]

    def core_copy(q):
        return pltpu.make_async_remote_copy(
            src_ref=core_send.at[q], dst_ref=core_recv.at[q],
            send_sem=core_ssem.at[q], recv_sem=core_rsem.at[q],
            device_id=(bat, sibling), device_id_type=MESH,
        )

    def core_go(q):
        core_send[q] = own_rows(1 - core, q).astype(BF)
        core_copy(q).start()

    def bat_copy(q, to, frm):
        return pltpu.make_async_remote_copy(
            src_ref=bat_send.at[q, to], dst_ref=bat_recv.at[q, frm],
            send_sem=bat_ssem.at[q, to], recv_sem=bat_rsem.at[q, frm],
            device_id=(to, me), device_id_type=MESH,
        )

    def bat_go(q):
        core_copy(q).wait_recv()
        part = own_rows(core, q) + core_recv[q].astype(F32)
        part_bat[q] = part.reshape(batches, rows_b, wide)
        bat_send[q] = part.astype(BF).reshape(batches, rows_b, wide)

        def go(k, carry):
            bat_copy(q, lax.rem(bat + k, batches), bat).start()
            return carry

        lax.fori_loop(1, batches, go, 0, unroll=depth <= 4)

    split_z = rows_z < rows_b

    def z_copy(q, to, frm):
        if split_z:
            src = z_send.at[q, pl.ds(to * rows_z, rows_z), :]
            dst = z_recv.at[q, frm, pl.ds(0, rows_z), :]
        else:
            src, dst = z_send.at[q], z_recv.at[q, frm]
        return pltpu.make_async_remote_copy(
            src_ref=src, dst_ref=dst, send_sem=z_ssem.at[q, to], recv_sem=z_rsem.at[q, frm],
            device_id=(bat, 2 * to + core), device_id_type=MESH,
        )

    def bat_add(q):
        def add(k, carry):
            frm = lax.rem(bat - k + batches, batches)
            bat_copy(q, frm, frm).wait_recv()
            part_bat[q, bat] += bat_recv[q, frm].astype(F32)
            return carry

        lax.fori_loop(1, batches, add, 0, unroll=depth <= 4)
        z_send[q] = part_bat[q, bat].astype(BF)

        def go(k, carry):
            z_copy(q, lax.rem(z + k, depth), z).start()
            return carry

        lax.fori_loop(1, depth, go, 0, unroll=depth <= 4)
        if split_z:
            z_recv[q, z, 0:rows_z, :] = z_send[q, pl.ds(pl.multiple_of(z * rows_z, rows_z), rows_z), :]
        else:
            z_recv[q, z] = z_send[q]

    def gz_copy(q, to, frm):
        spot = full.at[q, core, bat, pl.ds(frm * rows_z, rows_z), :]
        return pltpu.make_async_remote_copy(
            src_ref=spot, dst_ref=spot,
            send_sem=gz_ssem.at[q, to], recv_sem=gz_rsem.at[q, frm],
            device_id=(bat, 2 * to + core), device_id_type=MESH,
        )

    def z_sum(q):
        def wait(k, carry):
            frm = lax.rem(z - k + depth, depth)
            z_copy(q, frm, frm).wait_recv()
            return carry

        lax.fori_loop(1, depth, wait, 0, unroll=depth <= 4)
        rows = rows_z if split_z else rows_b
        summed = z_recv[q, 0, 0:rows, :].astype(F32)
        for other in range(1, depth):
            summed += z_recv[q, other, 0:rows, :].astype(F32)
        summed = summed.astype(BF)
        if split_z:
            full[q, core, bat, pl.ds(pl.multiple_of(z * rows_z, rows_z), rows_z), :] = summed

            def go(k, carry):
                gz_copy(q, lax.rem(z + k, depth), z).start()
                return carry

            lax.fori_loop(1, depth, go, 0, unroll=depth <= 4)
        else:
            full[q, core, bat] = summed

    def gbat_copy(q, to, frm):
        return pltpu.make_async_remote_copy(
            src_ref=full.at[q, core, frm], dst_ref=full.at[q, core, frm],
            send_sem=gbat_ssem.at[q, to], recv_sem=gbat_rsem.at[q, frm],
            device_id=(to, me), device_id_type=MESH,
        )

    def gbat_go(q):
        if split_z:

            def wait(k, carry):
                frm = lax.rem(z - k + depth, depth)
                gz_copy(q, frm, frm).wait_recv()
                return carry

            lax.fori_loop(1, depth, wait, 0, unroll=depth <= 4)

        def go(k, carry):
            gbat_copy(q, lax.rem(bat + k, batches), bat).start()
            return carry

        lax.fori_loop(1, batches, go, 0, unroll=depth <= 4)

    def gcore_copy(q, side):
        return pltpu.make_async_remote_copy(
            src_ref=full.at[q, side], dst_ref=full.at[q, side],
            send_sem=gcore_ssem.at[q], recv_sem=gcore_rsem.at[q],
            device_id=(bat, sibling), device_id_type=MESH,
        )

    def gcore_go(q):
        def wait(k, carry):
            frm = lax.rem(bat - k + batches, batches)
            gbat_copy(q, frm, frm).wait_recv()
            return carry

        lax.fori_loop(1, batches, wait, 0, unroll=depth <= 4)
        gcore_copy(q, core).start()

    pl.when(at_end)(functools.partial(front, last))
    for q in range(groups):
        pl.when(at_end)(functools.partial(add_total, last, q))
        core_go(q)
        if q > 0:
            bat_go(q - 1)
    pl.when(at_end)(functools.partial(back, last, QUEUE))
    bat_go(groups - 1)

    pl.when(at_end)(functools.partial(net_side, last))

    nsum_copy = pltpu.make_async_remote_copy(
        src_ref=net_send, dst_ref=net_recv, send_sem=nsum_sem.at[0], recv_sem=nsum_sem.at[1],
        device_id=(bat, sibling), device_id_type=MESH,
    )
    net_send[...] = net_sum[1 - core].astype(BF)
    nsum_copy.start()

    def add_and_pass(t, c, upward):
        rows = pl.ds(pl.multiple_of(c * grad_rows, grad_rows), grad_rows)
        grad_copy(t, c, upward).wait_recv()
        came = grad_in[t + 1 if upward else t, rows, :]
        grad_send[t, rows, :] = (own_grad[t, rows, :] + came.astype(F32)).astype(grad_send.dtype)
        grad_copy(t, c, upward).start()

    def pass_on(tick, carry):
        at = tick - LAG * z
        t = at // grad_chunks

        @pl.when((z > 0) & (t > z) & (t < depth))
        def _():
            add_and_pass(t, lax.rem(at, grad_chunks), True)

        at_down = tick - LAG * (depth - 1 - z)
        t_down = depth - 1 - at_down // grad_chunks

        @pl.when((z < depth - 1) & (t_down < z) & (t_down >= 0))
        def _():
            add_and_pass(t_down, lax.rem(at_down, grad_chunks), False)

        return carry

    first_tick = LAG + 2 * grad_chunks
    last_tick = (depth - 1) * grad_chunks + LAG
    end_tick = depth * grad_chunks + LAG * (depth - 2)
    lax.fori_loop(first_tick, last_tick, pass_on, 0)

    def ticks(frm, to):
        span = end_tick - last_tick
        lax.fori_loop(last_tick + span * frm // 6, last_tick + span * to // 6, pass_on, 0)

    def ticks(part):
        span, parts = end_tick - last_tick, 2 * groups
        lax.fori_loop(last_tick + span * part // parts, last_tick + span * (part + 1) // parts, pass_on, 0)

    for i in range(max(groups, grad_chunks - QUEUE)):
        if i + QUEUE < grad_chunks:
            end_more(last, i + QUEUE)
        if i < groups:
            bat_add(i)
    for q in range(groups):
        ticks(q)
        z_sum(q)
    for q in range(groups):
        gbat_go(q)
        ticks(groups + q)
    for q in range(groups):
        gcore_go(q)

    net_copy(core).wait_send()
    nsum_copy.wait_send()

    def drain_tab(t, carry):
        for c in range(tab_chunks):

            @pl.when(jnp.logical_and(t <= z, has_up))
            def _():
                tab_copy(t, c, True).wait_send()

            @pl.when(jnp.logical_and(t >= z, has_down))
            def _():
                tab_copy(t, c, False).wait_send()

        return carry

    lax.fori_loop(0, depth, drain_tab, 0)

    def drain_batch(k, carry):
        to = lax.rem(bat + k, batches)
        for q in range(groups):
            bat_copy(q, to, bat).wait_send()
        return carry

    def drain_z(k, carry):
        to = lax.rem(z + k, depth)
        code_copy(to, z).wait_send()
        for q in range(groups):
            z_copy(q, to, z).wait_send()
        return carry

    lax.fori_loop(1, batches, drain_batch, 0)
    lax.fori_loop(1, depth, drain_z, 0)
    for q in range(groups):
        core_copy(q).wait_send()

    nsum_copy.wait_recv()
    net_out[...] = net_sum[core] + net_recv[...].astype(F32)
    cell_out[...] = own_grad[z]

    @pl.when(has_down)
    def _():
        for c in range(grad_chunks):
            grad_copy(z, c, True).wait_recv()
        cell_out[...] += grad_in[z + 1].astype(F32)

    @pl.when(has_up)
    def _():
        for c in range(grad_chunks):
            grad_copy(z, c, False).wait_recv()
        cell_out[...] += grad_in[z].astype(F32)

    def drain_grad(t, carry):
        for c in range(grad_chunks):

            @pl.when((t != z) & jnp.logical_not(at_end & (t == last) & (c < grad_chunks - QUEUE)))
            def _():
                grad_copy(t, c, True).wait_send()

        return carry

    lax.fori_loop(0, depth, drain_grad, 0)

    def drain_gbat(k, carry):
        for q in range(groups):
            gbat_copy(q, lax.rem(bat + k, batches), bat).wait_send()
        return carry

    def drain_gz(k, carry):
        for q in range(groups):
            if split_z:
                gz_copy(q, lax.rem(z + k, depth), z).wait_send()
        return carry

    lax.fori_loop(1, batches, drain_gbat, 0)
    lax.fori_loop(1, depth, drain_gz, 0)
    for q in range(groups):
        gcore_copy(q, core).wait_send()

    for q in range(groups):
        gcore_copy(q, 1 - core).wait_recv()


def finish(scale, cell_sum, net_sum, full, cell_out, net_out, first_out, second_out, first, second, sem):
    groups, rows, wide = full.shape
    copies = [
        pltpu.make_async_copy(cell_sum, cell_out, sem.at[0, 0]), pltpu.make_async_copy(net_sum, net_out, sem.at[0, 1]),
    ]
    for copy in copies:
        copy.start()
    parts = sem.shape[1]
    for i in range(parts):
        part = slice(i * rows // parts, (i + 1) * rows // parts)
        for q in range(groups - 1):
            first[part, q * wide : (q + 1) * wide] = full[q, part, :].astype(F32) * scale
        second[part, :] = full[groups - 1, part, :].astype(F32) * scale
        for j, (a, b) in enumerate(((first, first_out), (second, second_out))):
            copies.append(pltpu.make_async_copy(a.at[part, :], b.at[part, :], sem.at[1 + j, i]))
            copies[-1].start()
    for copy in copies:
        copy.wait()


def on_device(cell_feat, net_feat, net_grad, w_first, w_second, pin_cell, pin_net, pin_count):
    owners = lax.axis_size("dom")
    batches = lax.axis_size("batch")
    cell, net, grad = cell_feat[0], net_feat[0], net_grad[0]
    capacity = pin_cell.shape[3]
    cells, feat = cell.shape
    nets = net.shape[0]
    fan_in, mid = w_first.shape
    groups = mid // feat + 1
    depth = owners // 2
    scale = 1.0 / math.sqrt(batches * owners * owners * capacity)
    half = fan_in // 2
    rows_b = half // batches
    split_z = rows_b // depth >= 16
    rows_z = rows_b // depth if split_z else rows_b
    slots = 2 * capacity
    wire = BF if depth <= 4 else F32
    dma = pltpu.SemaphoreType.DMA
    vmem = pltpu.VMEM
    hbm = pl.BlockSpec(memory_space=pltpu.HBM)
    on_chip = pl.BlockSpec(memory_space=pltpu.VMEM)

    cell_sum, net_sum, full = pl.pallas_call(
        functools.partial(kernel, batches, depth, rows_z),
        out_shape=(
            vmem((cells, feat), F32),
            vmem((nets, feat), F32),
            vmem((groups, 2, batches, rows_b, feat), BF),
        ),
        in_specs=[hbm] * 8,
        out_specs=[on_chip] * 3,
        scratch_shapes=[
            vmem((cells, feat), BF),
            vmem((nets, feat), BF),
            vmem((nets, feat), BF),
            vmem((fan_in, mid), BF),
            vmem((mid, feat), BF),
            vmem((owners, capacity), jnp.int32),
            vmem((owners, capacity), jnp.int32),
            pltpu.SMEM((1, owners), jnp.int32),
            vmem((depth, 2, slots), jnp.int32),
            vmem((depth, 2, slots), jnp.int32),
            vmem((depth, feat, cells), BF),
            vmem((2, 2 * feat, nets), BF),
            vmem((mid, fan_in), BF),
            vmem((depth, cells, slots), BF),
            vmem((depth, nets, slots), BF),
            vmem((feat, slots), BF),
            vmem((mid, slots), BF),
            vmem((depth, feat, slots), BF),
            vmem((depth, feat, slots), BF),
            vmem((depth, mid, slots), F32),
            vmem((depth, mid, slots), F32),
            vmem((depth, mid, slots), BF),
            vmem((groups, fan_in, feat), F32),
            vmem((depth, cells, feat), F32),
            vmem((depth, cells, feat), wire),
            vmem((depth + 1, cells, feat), wire),
            vmem((2, nets, feat), F32),
            vmem((nets, feat), BF),
            vmem((nets, feat), BF),
            vmem((groups, half, feat), BF),
            vmem((groups, half, feat), BF),
            vmem((groups, batches, rows_b, feat), BF),
            vmem((groups, batches, rows_b, feat), BF),
            vmem((groups, batches, rows_b, feat), F32),
            vmem((groups, rows_b, feat), BF),
            vmem((groups, depth, rows_b, feat), BF),
            dma((8,)),
            dma((depth,)), dma((depth,)), dma((2,)),
            dma((depth, TAB_CHUNKS)), dma((depth, TAB_CHUNKS)), dma((depth, TAB_CHUNKS)),
            dma((depth, GRAD_CHUNKS)), dma((depth + 1, GRAD_CHUNKS)), dma((2,)),
            dma((groups,)), dma((groups,)), dma((groups, batches)), dma((groups, batches)),
            dma((groups, depth)), dma((groups, depth)), dma((groups,)), dma((groups,)),
            dma((groups, batches)), dma((groups, batches)), dma((groups, depth)), dma((groups, depth)),
        ],
        compiler_params=pltpu.CompilerParams(
            collective_id=0, has_side_effects=True, vmem_limit_bytes=60 * 1024 * 1024
        ),
    )(cell, net, grad, w_first, w_second, pin_cell[0, 0], pin_net[0, 0], pin_count[0])
    cell_out, net_out, first, second = pl.pallas_call(
        functools.partial(finish, scale),
        out_shape=(
            jax.ShapeDtypeStruct((cells, feat), F32),
            jax.ShapeDtypeStruct((nets, feat), F32),
            jax.ShapeDtypeStruct((fan_in, mid), F32),
            jax.ShapeDtypeStruct((mid, feat), F32),
        ),
        in_specs=[on_chip] * 3,
        out_specs=[hbm] * 4,
        scratch_shapes=[vmem((fan_in, mid), F32), vmem((mid, feat), F32), dma((3, 2))],
    )(*(pltpu.with_memory_space_constraint(x, pltpu.VMEM) for x in (cell_sum, net_sum, full.reshape(groups, fan_in, feat))))
    return (cell_out[None], net_out[None], first, second)


def solution(mesh):
    return jax.shard_map(
        on_device,
        mesh=mesh,
        in_specs=(
            P("batch", "dom", None),
            P("batch", "dom", None),
            P("batch", "dom", None),
            P(),
            P(),
            P("batch", "dom", None, None),
            P("batch", "dom", None, None),
            P("batch", "dom", None),
        ),
        out_specs=(P("batch", "dom", None), P("batch", "dom", None), P(), P()),
        check_vma=False,
    )
```
